256 devices in a mesh: snap: 8 (over x, core), slab: 32 (over y, z).
Axes of the slice: x: 4, y: 4, z: 8, core: 2. Of those that a mesh axis runs over, the one named last changes fastest.
Arguments:
- velocity: bfloat16 [256, 3, 160, 8, 128], P('snap', None, 'slab'), may hold values from -10 to 10
Outputs:
- modes: bfloat16 [768, 32, 5120], P(None, 'slab', 'snap')
- factor: float32 [768, 768], replicated
The draws below stay inside these ranges and needn't reach their ends.
All inputs are finite; a program needn't handle non-finite values.
Results may differ from the reference program's by a relative error of at most 0.0004.
The reference program's roundings to bfloat16 on the way count: a program that leaves them out, or rounds other values in their place, can miss the bound.
Values may be sent and summed in bfloat16 or wider, within the bound.
No kernel may reach another device: no remote copies, remote signals or barrier semaphores. Data moves between devices by JAX's collectives and lax.ppermute only.
A program may use at most 64 MiB of HBM per device.

```python
import math
import jax
import jax.numpy as jnp
from jax import lax

SNAPS = 256
CX = 5
Y = 8
Z = 128
NX = 160
POINTS = 163840
N_SLAB = 32


def draw_velocity(key, part):
    groups = SNAPS // 4
    amp_x = 0.5 + jnp.arange(NX, dtype=jnp.float32) / NX
    scale_key = jax.random.fold_in(key, 7)
    amp_s = jnp.exp(jax.random.uniform(scale_key, (SNAPS,), minval=math.log(0.6), maxval=math.log(1.6)))

    def one_group(index):
        group_key = jax.random.fold_in(key, index + 11)
        key_own, key_shared = jax.random.split(group_key)
        own = jnp.clip(jax.random.normal(key_own, (4, 3, NX, Y, Z)), -4.0, 4.0)
        shared = jnp.clip(jax.random.normal(key_shared, (1, 3, NX, Y, Z)), -4.0, 4.0)
        scales = lax.dynamic_slice_in_dim(amp_s, index * 4, 4, 0)
        field = (own + 0.7 * shared) * amp_x[None, None, :, None, None]
        field = field * scales[:, None, None, None, None] * 0.6
        return field.astype(jnp.bfloat16)
    drawn = lax.map(one_group, jnp.arange(groups, dtype=jnp.int32))
    return drawn.reshape(SNAPS, 3, NX, Y, Z)


def setup_inputs(seed: int = 0) -> dict:
    streams_of = jax.random.split(jax.random.key(seed), 2)
    return {
        "velocity": draw_velocity(jax.random.fold_in(streams_of[1], 71), 0),
    }


stencil_weights = (4.0 / 5.0, -1.0 / 5.0, 4.0 / 105.0, -1.0 / 280.0)

def differ(padded, axis, length):
    total = None
    for offset in range(4):
        step = offset + 1
        ahead = lax.slice_in_dim(padded, 4 + step, 4 + step + length, axis=axis)
        behind = lax.slice_in_dim(padded, 4 - step, 4 - step + length, axis=axis)
        term = stencil_weights[offset] * (ahead - behind)
        total = term if total is None else total + term
    return total

def derive(field, axis):
    widths = [(0, 0)] * field.ndim
    widths[axis] = (4, 4)
    return differ(jnp.pad(field, widths), axis, field.shape[axis])

def vorticity_of(snapshot):
    field = snapshot.astype(jnp.float32)
    first, second, third = (field[0], field[1], field[2])
    omega_one = derive(third, 1) - derive(second, 2)
    omega_two = derive(first, 2) - derive(third, 0)
    omega_three = derive(second, 0) - derive(first, 1)
    return jnp.stack([omega_one, omega_two, omega_three], axis=0).astype(jnp.bfloat16)

def reference(velocity):
    vorticity = lax.map(vorticity_of, velocity)
    width = 3 * SNAPS
    planes = vorticity.reshape(width, NX, Y * Z)

    def add_plane(index, total):
        plane = lax.dynamic_slice_in_dim(planes, index, 1, 1)[:, 0, :]
        return total + jnp.dot(plane.astype(jnp.float32), plane.T.astype(jnp.float32), preferred_element_type=jnp.float32)
    gram = lax.fori_loop(0, NX, add_plane, jnp.zeros((width, width), jnp.float32))
    lower = jnp.linalg.cholesky(gram / POINTS)
    factor = lower.T

    def solve_plane(index, result):
        plane = lax.dynamic_slice_in_dim(planes, index, 1, 1)[:, 0, :]
        block = jax.scipy.linalg.solve_triangular(lower, plane.astype(jnp.float32), lower=True)
        return lax.dynamic_update_slice_in_dim(result, block.astype(jnp.bfloat16)[:, None, :], index, 1)
    solved = lax.fori_loop(0, NX, solve_plane, jnp.zeros((width, NX, Y * Z), jnp.bfloat16))
    modes = solved.reshape(width, N_SLAB, CX * Y * Z)
    return (modes, factor)
```

```python
import jax
import jax.numpy as jnp
from jax import lax
from jax.experimental import pallas as pl
from jax.experimental.pallas import tpu as pltpu
from jax.sharding import Mesh, PartitionSpec as P

weights = (4.0 / 5.0, -1.0 / 5.0, 4.0 / 105.0, -1.0 / 280.0)
POINTS = 163840
NB = 6
S = 128
F32 = jnp.float32
BF16 = jnp.bfloat16
VM = pl.BlockSpec(memory_space=pltpu.VMEM)


def ramp(field, axis, coeffs):
    total = None
    for shift, coeff in coeffs:
        term = coeff * pltpu.roll(field, shift, axis)
        total = term if total is None else total + term
    return total


def vort_kernel(vel, lo, hi, out, buf):
    shape = (5, 8, 128)
    y = lax.broadcasted_iota(jnp.int32, shape, 1)
    z = lax.broadcasted_iota(jnp.int32, shape, 2)
    ycs = []
    for r in range(1, 8):
        up = jnp.where(y + r < 8, weights[r - 1] if r <= 4 else 0.0, 0.0)
        down = jnp.where(y + r >= 8, weights[7 - r] if r >= 4 else 0.0, 0.0)
        ycs.append((8 - r, (up - down).astype(F32)))
    zcs = []
    for k in range(1, 5):
        zcs.append((128 - k, jnp.where(z + k < 128, weights[k - 1], 0.0).astype(F32)))
        zcs.append((k, jnp.where(z >= k, -weights[k - 1], 0.0).astype(F32)))

    def along_x(parts):
        planes = jnp.concatenate(parts, axis=0)
        total = None
        for k in range(1, 5):
            term = weights[k - 1] * (planes[4 + k : 9 + k] - planes[4 - k : 9 - k])
            total = term if total is None else total + term
        return total

    def one(s, carry):
        u = vel[s, 0].astype(F32)
        v = vel[s, 1].astype(F32)
        w = vel[s, 2].astype(F32)
        dxv = along_x([lo[s, 0].astype(F32), v, hi[s, 0].astype(F32)])
        dxw = along_x([lo[s, 1].astype(F32), w, hi[s, 1].astype(F32)])
        one_ = ramp(w, 1, ycs) - ramp(v, 2, zcs)
        two_ = ramp(u, 2, zcs) - dxw
        three_ = dxv - ramp(u, 1, ycs)
        for c, o in enumerate((one_, two_, three_)):
            buf[pl.ds(pl.multiple_of((s * 3 + c) * 40, 8), 40), :] = o.reshape(40, 128)
        return carry

    lax.fori_loop(0, 32, one, 0)
    for p in range(40):
        out[p // 5, :, (p % 5) * 128 : (p % 5 + 1) * 128] = buf[pl.ds(p, 96, stride=40), :].astype(BF16)


def vorticity(vel, lo, hi):
    return pl.pallas_call(
        vort_kernel,
        out_shape=jax.ShapeDtypeStruct((8, 96, 640), BF16),
        in_specs=[VM, VM, VM],
        out_specs=VM,
        scratch_shapes=[pltpu.VMEM((96 * 40, 128), F32)],
        compiler_params=pltpu.CompilerParams(vmem_limit_bytes=32 << 20),
    )(vel, lo, hi)


def block(K, J):
    return K * NB - K * (K - 1) // 2 + (J - K)


def gram_kernel(m, out):
    for K in range(NB):
        rows = m[K * S : K * S + S, :]
        res = lax.dot_general(rows, m[K * S :, :], (((1,), (1,)), ((), ())), preferred_element_type=F32)
        for J in range(K, NB):
            b = block(K, J)
            out[b * S : b * S + S, :] = res[:, (J - K) * S : (J - K + 1) * S]
    out[21 * S :, :] = jnp.zeros((S, S), F32)


def gram_blocks(m):
    return pl.pallas_call(
        gram_kernel,
        out_shape=jax.ShapeDtypeStruct((22 * S, S), F32),
        in_specs=[VM],
        out_specs=VM,
        compiler_params=pltpu.CompilerParams(vmem_limit_bytes=32 << 20),
    )(m)


SWAP = [(0, 1), (1, 0)]


def scatter_core(v):
    i = lax.axis_index("c")
    h = v.shape[0] // 2
    send = lax.dynamic_slice_in_dim(v, (1 - i) * h, h, 0)
    keep = lax.dynamic_slice_in_dim(v, i * h, h, 0)
    return keep + lax.ppermute(send, "c", SWAP)


def gather_core(v):
    i = lax.axis_index("c")
    o = lax.ppermute(v, "c", SWAP)
    return jnp.concatenate([jnp.where(i == 0, v, o), jnp.where(i == 0, o, v)], 0)


def ring(n, k):
    return [(j, (j + k) % n) for j in range(n)]


def scatter_x(v):
    i = lax.axis_index("x")
    h = v.shape[0] // 4
    total = lax.dynamic_slice_in_dim(v, i * h, h, 0)
    got = []
    for k in (2, 1, 3):
        send = lax.dynamic_slice_in_dim(v, ((i + k) % 4) * h, h, 0)
        got.append(lax.ppermute(send, "x", ring(4, k)))
    for g in got:
        total = total + g
    return total


def gather_x(v):
    i = lax.axis_index("x")
    h = v.shape[0]
    parts = {0: v}
    for k in (2, 1, 3):
        parts[k] = lax.ppermute(v, "x", ring(4, k))
    out = jnp.zeros((4 * h,) + v.shape[1:], v.dtype)
    for k in range(4):
        out = lax.dynamic_update_slice_in_dim(out, parts[k], ((i - k) % 4) * h, 0)
    return out


def scatter_yz(v):
    got = lax.all_to_all(v.reshape(32, -1, v.shape[1]), ("y", "z"), 0, 0, tiled=True)
    return got.sum(0)


def gather_yz(v):
    got = lax.all_to_all(jnp.broadcast_to(v[None], (32,) + v.shape), ("y", "z"), 0, 0, tiled=True)
    return got.reshape(-1, v.shape[1])


def total_of(v):
    share = scatter_yz(scatter_x(scatter_core(v))) / POINTS
    return gather_core(gather_x(gather_yz(share)))


HI = lax.Precision.HIGHEST


def dot_t(a, b):
    return lax.dot_general(a, b, (((0,), (0,)), ((), ())), precision=HI, preferred_element_type=F32)


def dot(a, b):
    return lax.dot_general(a, b, (((1,), (0,)), ((), ())), precision=HI, preferred_element_type=F32)


def lane(v, i):
    return jnp.broadcast_to(v[:, i : i + 1], (8, 128))


def sub(v, i):
    return jnp.broadcast_to(v[i : i + 1, :], (8, 128))


def diag(D, T):
    rows = lax.broadcasted_iota(jnp.int32, (8, 128), 0)
    lanes = lax.broadcasted_iota(jnp.int32, (8, 128), 1)
    for g in range(16):
        T[8 * g : 8 * g + 8, :] = (rows + 8 * g == lanes).astype(F32)
    for g in range(16):
        Dg = D[8 * g : 8 * g + 8, :]
        Wg = T[8 * g : 8 * g + 8, :]
        B = [lane(Dg, 8 * g + m) for m in range(8)]
        d = {(i, m): sub(B[m], i) for m in range(8) for i in range(m, 8)}
        inv = [None] * 8
        F = [None] * 8
        dm = {}
        for s in range(8):
            inv[s] = 1.0 / d[s, s]
            for i in range(s + 1, 8):
                dm[i, s] = d[i, s]
            F[s] = jnp.where(rows > s, B[s] * inv[s], 0.0)
            for m in range(s + 1, 8):
                B[m] = B[m] - F[s] * d[m, s]
                for i in range(m, 8):
                    d[i, m] = d[i, m] - (d[i, s] * d[m, s]) * inv[s]
        pivots = d[7, 7]
        for s in range(7):
            pivots = jnp.where(rows == s, d[s, s], pivots)
        scale = lax.rsqrt(pivots)
        U = []
        V = []
        for s in range(8):
            u = sub(Dg, s)
            v = sub(Wg, s)
            U.append(u)
            V.append(v)
            Dg = Dg - F[s] * u
            Wg = Wg - F[s] * v
        D[8 * g : 8 * g + 8, :] = jnp.where(lanes >= rows + 8 * g, Dg * scale, 0.0)
        T[8 * g : 8 * g + 8, :] = Wg * scale
        for h in range(g + 1, 16):
            Dh = D[8 * h : 8 * h + 8, :]
            Wh = T[8 * h : 8 * h + 8, :]
            Bh = [lane(Dh, 8 * g + m) for m in range(8)]
            for s in range(8):
                f = Bh[s] * inv[s]
                for m in range(s + 1, 8):
                    Bh[m] = Bh[m] - f * dm[m, s]
                Dh = Dh - f * U[s]
                Wh = Wh - f * V[s]
            D[8 * h : 8 * h + 8, :] = Dh
            T[8 * h : 8 * h + 8, :] = Wh


def chol_kernel(a, m, f, x, A, T, M, X):
    for K in range(NB):
        for J in range(K):
            f[K * S : K * S + S, J * S : J * S + S] = jnp.zeros((S, S), F32)

    def entry(K, b):
        return a[b * S : b * S + S, :] if K == 0 else A[b]

    for K in range(NB):
        D = A.at[block(K, K)]
        if K == 0:
            D[...] = a[0:S, :]
        diag(D, T)
        f[K * S : K * S + S, K * S : K * S + S] = D[...]
        t = T[...]
        for J in range(K + 1, NB):
            f[K * S : K * S + S, J * S : J * S + S] = dot(t, entry(K, block(K, J)))
        mk = m[K * S : K * S + S, :].astype(F32) if K == 0 else M[K * S : K * S + S, :]
        xk = dot(t, mk)
        X[...] = xk
        x[K * S : K * S + S, :] = xk.astype(BF16)
        for I in range(K + 1, NB):
            r = f[K * S : K * S + S, I * S : I * S + S]
            for J in range(I, NB):
                b = block(I, J)
                A[b] = entry(K, b) - dot_t(r, f[K * S : K * S + S, J * S : J * S + S])
            m0 = m[I * S : I * S + S, :].astype(F32) if K == 0 else M[I * S : I * S + S, :]
            M[I * S : I * S + S, :] = m0 - dot_t(r, X[...])


def chol_solve(blocks, m):
    n = m.shape[1]
    return pl.pallas_call(
        chol_kernel,
        out_shape=(jax.ShapeDtypeStruct((NB * S, NB * S), F32), jax.ShapeDtypeStruct((NB * S, n), BF16)),
        in_specs=[VM, VM],
        out_specs=(VM, VM),
        scratch_shapes=[
            pltpu.VMEM((21, S, S), F32),
            pltpu.VMEM((S, S), F32),
            pltpu.VMEM((NB * S, n), F32),
            pltpu.VMEM((S, n), F32),
        ],
        compiler_params=pltpu.CompilerParams(vmem_limit_bytes=40 << 20),
    )(blocks, m)


def body(velocity):
    slabs = 32
    forward = [(i, i + 1) for i in range(slabs - 1)]
    backward = [(i + 1, i) for i in range(slabs - 1)]
    lo = lax.ppermute(velocity[:, 1:, 1:5], ("y", "z"), forward)
    hi = lax.ppermute(velocity[:, 1:, 0:4], ("y", "z"), backward)
    shares = vorticity(velocity, lo, hi)
    got = lax.all_to_all(shares, ("x", "c"), 0, 0, tiled=True)
    matrix = got.reshape(NB * S, 640)
    total = total_of(gram_blocks(matrix))
    factor, modes = chol_solve(total, matrix)
    return modes.reshape(NB * S, 1, 640), factor


def solution(mesh):
    fine = Mesh(mesh.devices.reshape(4, 2, 4, 8), ("x", "c", "y", "z"))
    in_specs = (P(("x", "c"), None, ("y", "z"), None, None),)
    out_specs = (P(None, ("y", "z"), ("x", "c")), P())
    return jax.shard_map(body, mesh=fine, in_specs=in_specs, out_specs=out_specs, check_vma=False)
```

```python
import jax
import jax.numpy as jnp
from jax import lax
from jax.experimental import pallas as pl
from jax.experimental.pallas import tpu as pltpu
from jax.sharding import Mesh, PartitionSpec as P

weights = (4.0 / 5.0, -1.0 / 5.0, 4.0 / 105.0, -1.0 / 280.0)
POINTS = 163840
NB = 6
S = 128
F32 = jnp.float32
BF16 = jnp.bfloat16
VM = pl.BlockSpec(memory_space=pltpu.VMEM)


def ramp(field, axis, coeffs):
    total = None
    for shift, coeff in coeffs:
        term = coeff * pltpu.roll(field, shift, axis)
        total = term if total is None else total + term
    return total


def tables():
    shape = (5, 8, 128)
    y = lax.broadcasted_iota(jnp.int32, shape, 1)
    z = lax.broadcasted_iota(jnp.int32, shape, 2)
    ycs = []
    for r in range(1, 8):
        up = jnp.where(y + r < 8, weights[r - 1] if r <= 4 else 0.0, 0.0)
        down = jnp.where(y + r >= 8, weights[7 - r] if r >= 4 else 0.0, 0.0)
        ycs.append((8 - r, (up - down).astype(F32)))
    zcs = []
    for k in range(1, 5):
        zcs.append((128 - k, jnp.where(z + k < 128, weights[k - 1], 0.0).astype(F32)))
        zcs.append((k, jnp.where(z >= k, -weights[k - 1], 0.0).astype(F32)))
    return ycs, zcs


def along_x(parts):
    planes = jnp.concatenate(parts, axis=0)
    total = None
    for k in range(1, 5):
        term = weights[k - 1] * (planes[4 + k : 9 + k] - planes[4 - k : 9 - k])
        total = term if total is None else total + term
    return total


def emit(buf, out, rows):
    for p in range(40):
        out[p // 5, :, (p % 5) * 128 : (p % 5 + 1) * 128] = buf[pl.ds(p, rows, stride=40), :].astype(BF16)


def place(buf, row, value):
    buf[pl.ds(pl.multiple_of(row * 40, 8), 40), :] = value.reshape(40, 128)


def inner_kernel(vel, out, rest, buf):
    ycs, zcs = tables()

    def one(s, carry):
        u = vel[s, 0].astype(F32)
        v = vel[s, 1].astype(F32)
        w = vel[s, 2].astype(F32)
        place(buf, s, ramp(w, 1, ycs) - ramp(v, 2, zcs))
        rest[0, s] = ramp(u, 2, zcs)
        rest[1, s] = ramp(u, 1, ycs)
        return carry

    lax.fori_loop(0, 32, one, 0)
    emit(buf, out, 32)


def outer_kernel(vel, lo, hi, rest, out, buf):
    def one(s, carry):
        v = vel[s, 1].astype(F32)
        w = vel[s, 2].astype(F32)
        dxv = along_x([lo[s, 0].astype(F32), v, hi[s, 0].astype(F32)])
        dxw = along_x([lo[s, 1].astype(F32), w, hi[s, 1].astype(F32)])
        place(buf, s, rest[0, s] - dxw)
        place(buf, 32 + s, dxv - rest[1, s])
        return carry

    lax.fori_loop(0, 32, one, 0)
    emit(buf, out, 64)


def inner(vel):
    return pl.pallas_call(
        inner_kernel,
        out_shape=(jax.ShapeDtypeStruct((8, 32, 640), BF16), jax.ShapeDtypeStruct((2, 32, 5, 8, 128), F32)),
        in_specs=[VM],
        out_specs=(VM, VM),
        scratch_shapes=[pltpu.VMEM((32 * 40, 128), F32)],
        compiler_params=pltpu.CompilerParams(vmem_limit_bytes=16 << 20),
        cost_estimate=pl.CostEstimate(flops=10_000_000, bytes_accessed=12_000_000, transcendentals=0),
    )(vel)


def outer(vel, lo, hi, rest):
    return pl.pallas_call(
        outer_kernel,
        out_shape=jax.ShapeDtypeStruct((8, 64, 640), BF16),
        in_specs=[VM] * 4,
        out_specs=VM,
        scratch_shapes=[pltpu.VMEM((64 * 40, 128), F32)],
        compiler_params=pltpu.CompilerParams(vmem_limit_bytes=16 << 20),
        cost_estimate=pl.CostEstimate(flops=10_000_000, bytes_accessed=6_000_000, transcendentals=0),
    )(vel, lo, hi, rest)


def block(K, J):
    return K * NB - K * (K - 1) // 2 + (J - K)


def gram_kernel(one, two, m, out, buf):
    for j in range(5):
        cols = slice(j * 128, j * 128 + 128)
        for d in range(8):
            buf[j, pl.ds(96 * d, 32, stride=3), :] = one[d, :, cols].astype(F32)
            buf[j, pl.ds(96 * d + 1, 32, stride=3), :] = two[d, 0:32, cols].astype(F32)
            buf[j, pl.ds(96 * d + 2, 32, stride=3), :] = two[d, 32:64, cols].astype(F32)
        m[:, cols] = buf[j].astype(BF16)
    for K in range(NB):
        rows = m[K * S : K * S + S, :]
        res = lax.dot_general(rows, m[K * S :, :], (((1,), (1,)), ((), ())), preferred_element_type=F32)
        for J in range(K, NB):
            b = block(K, J)
            out[b * S : b * S + S, :] = res[:, (J - K) * S : (J - K + 1) * S]
    out[21 * S :, :] = jnp.zeros((S, S), F32)


def gram_blocks(one, two):
    return pl.pallas_call(
        gram_kernel,
        out_shape=(jax.ShapeDtypeStruct((NB * S, 640), BF16), jax.ShapeDtypeStruct((22 * S, S), F32)),
        in_specs=[VM, VM],
        out_specs=(VM, VM),
        scratch_shapes=[pltpu.VMEM((5, NB * S, 128), F32)],
        compiler_params=pltpu.CompilerParams(vmem_limit_bytes=32 << 20),
    )(one, two)


SWAP = [(0, 1), (1, 0)]


def scatter_core(v):
    i = lax.axis_index("c")
    h = v.shape[0] // 2
    send = lax.dynamic_slice_in_dim(v, (1 - i) * h, h, 0)
    keep = lax.dynamic_slice_in_dim(v, i * h, h, 0)
    return keep + lax.ppermute(send, "c", SWAP)


def gather_core(v):
    i = lax.axis_index("c")
    o = lax.ppermute(v, "c", SWAP)
    return jnp.concatenate([jnp.where(i == 0, v, o), jnp.where(i == 0, o, v)], 0)


def ring(n, k):
    return [(j, (j + k) % n) for j in range(n)]


def scatter_x(v):
    i = lax.axis_index("x")
    h = v.shape[0] // 4
    total = lax.dynamic_slice_in_dim(v, i * h, h, 0)
    got = []
    for k in (2, 1, 3):
        send = lax.dynamic_slice_in_dim(v, ((i + k) % 4) * h, h, 0)
        got.append(lax.ppermute(send, "x", ring(4, k)))
    for g in got:
        total = total + g
    return total


def gather_x(v):
    i = lax.axis_index("x")
    h = v.shape[0]
    parts = {0: v}
    for k in (2, 1, 3):
        parts[k] = lax.ppermute(v, "x", ring(4, k))
    out = jnp.zeros((4 * h,) + v.shape[1:], v.dtype)
    for k in range(4):
        out = lax.dynamic_update_slice_in_dim(out, parts[k], ((i - k) % 4) * h, 0)
    return out


def scatter_yz(v):
    got = lax.all_to_all(v.reshape(32, -1, v.shape[1]), ("y", "z"), 0, 0, tiled=True)
    return got.sum(0)


def gather_yz(v):
    got = lax.all_to_all(jnp.broadcast_to(v[None], (32,) + v.shape), ("y", "z"), 0, 0, tiled=True)
    return got.reshape(-1, v.shape[1])


def total_of(v):
    share = scatter_yz(scatter_x(scatter_core(v))) / POINTS
    return gather_core(gather_x(gather_yz(share)))


BF=jnp.bfloat16
def parts(x):
    a=x.astype(BF); r=x-a.astype(jnp.float32)
    b=r.astype(BF); r=r-b.astype(jnp.float32)
    return a,b,r.astype(BF)
def left(p): a,b,c=p; return jnp.concatenate([a,a,b,a,b,c],axis=1)
def right(p): a,b,c=p; return jnp.concatenate([a,b,a,c,b,a],axis=0)
def mm(l,r): return lax.dot_general(l,r,(((1,),(0,)),((),())),preferred_element_type=jnp.float32)

def bi(K,J): return K*NB-K*(K-1)//2+(J-K)
def lane(v,i): return jnp.broadcast_to(v[:,i:i+1],(8,128))
def sub(v,i): return jnp.broadcast_to(v[i:i+1,:],(8,128))
NV=4
def diag(D,T,ones,fill):
    rows=lax.broadcasted_iota(jnp.int32,(8,128),0)
    lanes=lax.broadcasted_iota(jnp.int32,(8,128),1)
    one=ones[...]
    for g in range(16):
        T[8*g:8*g+8,:]=(rows+8*g==lanes).astype(jnp.float32)
    total=len(fill)
    for g in range(16):
        while fill and total-len(fill)<total*(g+1)//15:
            fill.pop(0)()
        Dg=D[8*g:8*g+8,:]; Wg=T[8*g:8*g+8,:]
        B=[lane(Dg,8*g+m)*one for m in range(8)]
        d={(i,m):sub(B[m],i) for m in range(8) for i in range(m,8)}
        inv=[None]*8; F=[None]*8
        dm={}
        for s in range(8):
            inv[s]=1.0/d[s,s]
            for i in range(s+1,8): dm[i,s]=d[i,s]
            F[s]=jnp.where(rows>s,B[s]*inv[s],0.0)
            for m in range(s+1,8):
                B[m]=B[m]-F[s]*d[m,s]
                for i in range(m,8):
                    d[i,m]=d[i,m]-(d[i,s]*d[m,s])*inv[s]
        piv=d[7,7]
        for s in range(7): piv=jnp.where(rows==s,d[s,s],piv)
        rsq=lax.rsqrt(piv)
        U=[];V=[]
        for s in range(8):
            u=sub(Dg,s); v=sub(Wg,s); U.append(u); V.append(v)
            Dg=Dg-F[s]*u; Wg=Wg-F[s]*v
        Rg=jnp.where(lanes>=rows+8*g,Dg*rsq,0.0); Tg=Wg*rsq
        D[8*g:8*g+8,:]=Rg
        T[8*g:8*g+8,:]=Tg
        for h in range(g+1,min(g+1+NV,16)):
            Dh=D[8*h:8*h+8,:]; Wh=T[8*h:8*h+8,:]
            Bh=[lane(Dh,8*g+m) for m in range(8)]
            for s in range(8):
                f=Bh[s]*inv[s]
                for m in range(s+1,8): Bh[m]=Bh[m]-f*dm[m,s]
                Dh=Dh-f*U[s]; Wh=Wh-f*V[s]
            D[8*h:8*h+8,:]=Dh; T[8*h:8*h+8,:]=Wh
        r0=8*(g+1+NV)
        if r0<128:
            p=[q.astype(jnp.float32) for q in parts(jnp.concatenate([Rg,Tg],axis=1))]
            rr=jnp.concatenate([p[0],p[1],p[0],p[2],p[1],p[0]],axis=0).astype(BF)
            ll=jnp.concatenate([p[i][:,:128] for i in (0,0,1,0,1,2)],axis=0)
            upd=mm(jnp.transpose(ll)[r0:,:].astype(BF),rr)
            D[r0:,:]=D[r0:,:]-upd[:,:128]
            T[r0:,:]=T[r0:,:]-upd[:,128:]
def kernel(a_ref,m_ref,ones,f_ref,x_ref,A,T,M,TP,RT,RP,XP):
    n=m_ref.shape[1]
    def zero():
        for K in range(NB):
            if K: f_ref[K*S:K*S+S,0:K*S]=jnp.zeros((S,K*S),jnp.float32)
    fill=[]
    def put(ref,p):
        for i in range(3): ref[i]=p[i]
    def get(ref): return ref[0],ref[1],ref[2]
    for K in range(NB):
        Dk=A.at[bi(K,K)]
        if K==0:
            Dk[...]=a_ref[0]
        diag(Dk,T,ones,fill)
        assert not fill
        f_ref[K*S:K*S+S,K*S:K*S+S]=Dk[...]
        put(TP,parts(T[...]))
        src=a_ref if K==0 else A
        def panel(J,K=K,src=src):
            r=mm(left(get(TP)),right(parts(src[bi(K,J)])))
            f_ref[K*S:K*S+S,J*S:J*S+S]=r
            put(RT.at[J],parts(jnp.transpose(r))); put(RP.at[J],parts(r))
        def update(I,J,K=K,src=src):
            b=bi(I,J)
            A[b]=src[b]-mm(left(get(RT.at[I])),right(get(RP.at[J])))
        def solve(K=K):
            tp=get(TP)
            if K==0:
                m=m_ref[K*S:K*S+S,:]
                xk=mm(jnp.concatenate(tp,axis=1),jnp.concatenate([m,m,m],axis=0))
            else:
                xk=mm(left(tp),right(parts(M[K*S:K*S+S,:])))
            x_ref[K*S:K*S+S,:]=xk.astype(BF)
            if K<NB-1: put(XP,parts(xk))
        def updm(I,K=K):
            m0=m_ref[I*S:I*S+S,:].astype(jnp.float32) if K==0 else M[I*S:I*S+S,:]
            M[I*S:I*S+S,:]=m0-mm(left(get(RT.at[I])),right(get(XP)))
        if K==NB-1:
            solve(); break
        panel(K+1)
        update(K+1,K+1)
        if K==0: fill.append(zero)
        for J in range(K+2,NB): fill.append(lambda J=J,f=panel: f(J))
        fill.append(solve)
        for I in range(K+1,NB):
            for J in range(I,NB):
                if J>K+1: fill.append(lambda I=I,J=J,f=update: f(I,J))
            fill.append(lambda I=I,f=updm: f(I))
def chol_solve(blocks,m):
    n=m.shape[1]
    vm=pl.BlockSpec(memory_space=pltpu.VMEM)
    return pl.pallas_call(kernel,out_shape=(jax.ShapeDtypeStruct((768,768),jnp.float32),jax.ShapeDtypeStruct((768,n),jnp.bfloat16)),
        in_specs=[vm,vm,vm],out_specs=(vm,vm),
        scratch_shapes=[pltpu.VMEM((21,S,S),jnp.float32),pltpu.VMEM((S,S),jnp.float32),pltpu.VMEM((768,n),jnp.float32),pltpu.VMEM((3,S,S),BF),pltpu.VMEM((NB,3,S,S),BF),pltpu.VMEM((NB,3,S,S),BF),pltpu.VMEM((3,S,n),BF)],
        compiler_params=pltpu.CompilerParams(vmem_limit_bytes=40<<20))(blocks,m,jnp.ones((8,128),jnp.float32))


def body(velocity):
    slabs = 32
    forward = [(i, i + 1) for i in range(slabs - 1)]
    backward = [(i + 1, i) for i in range(slabs - 1)]
    lo = lax.ppermute(velocity[:, 1:, 1:5], ("y", "z"), forward)
    hi = lax.ppermute(velocity[:, 1:, 0:4], ("y", "z"), backward)
    share, rest = inner(velocity)
    one = lax.all_to_all(share, ("x", "c"), 0, 0, tiled=True)
    two = lax.all_to_all(outer(velocity, lo, hi, rest), ("x", "c"), 0, 0, tiled=True)
    matrix, blocks = gram_blocks(one, two)
    total = total_of(blocks).reshape(22, S, S)
    factor, modes = chol_solve(total, matrix)
    return modes.reshape(NB * S, 1, 640), factor


def solution(mesh):
    fine = Mesh(mesh.devices.reshape(4, 2, 4, 8), ("x", "c", "y", "z"))
    in_specs = (P(("x", "c"), None, ("y", "z"), None, None),)
    out_specs = (P(None, ("y", "z"), ("x", "c")), P())
    return jax.shard_map(body, mesh=fine, in_specs=in_specs, out_specs=out_specs, check_vma=False)
```

```python
import jax
import jax.numpy as jnp
from jax import lax
from jax.experimental import pallas as pl
from jax.experimental.pallas import tpu as pltpu
from jax.sharding import Mesh, PartitionSpec as P

weights = (4.0 / 5.0, -1.0 / 5.0, 4.0 / 105.0, -1.0 / 280.0)
POINTS = 163840
NB = 6
S = 128
F32 = jnp.float32
BF16 = jnp.bfloat16
VM = pl.BlockSpec(memory_space=pltpu.VMEM)
HBM = pl.BlockSpec(memory_space=pltpu.MemorySpace.HBM)


def ramp(field, axis, coeffs):
    total = None
    for shift, coeff in coeffs:
        term = coeff * pltpu.roll(field, shift, axis)
        total = term if total is None else total + term
    return total


def tables():
    shape = (5, 8, 128)
    y = lax.broadcasted_iota(jnp.int32, shape, 1)
    z = lax.broadcasted_iota(jnp.int32, shape, 2)
    ycs = []
    for r in range(1, 8):
        up = jnp.where(y + r < 8, weights[r - 1] if r <= 4 else 0.0, 0.0)
        down = jnp.where(y + r >= 8, weights[7 - r] if r >= 4 else 0.0, 0.0)
        ycs.append((8 - r, (up - down).astype(F32)))
    zcs = []
    for k in range(1, 5):
        zcs.append((128 - k, jnp.where(z + k < 128, weights[k - 1], 0.0).astype(F32)))
        zcs.append((k, jnp.where(z >= k, -weights[k - 1], 0.0).astype(F32)))
    return ycs, zcs


def along_x(parts):
    planes = jnp.concatenate(parts, axis=0)
    total = None
    for k in range(1, 5):
        term = weights[k - 1] * (planes[4 + k : 9 + k] - planes[4 - k : 9 - k])
        total = term if total is None else total + term
    return total


def emit(buf, out, rows):
    for p in range(40):
        out[p // 5, :, (p % 5) * 128 : (p % 5 + 1) * 128] = buf[pl.ds(p, rows, stride=40), :].astype(BF16)


def place(buf, row, value):
    buf[pl.ds(pl.multiple_of(row * 40, 8), 40), :] = value.reshape(40, 128)


def inner_kernel(vel, out, rest, buf):
    ycs, zcs = tables()

    def one(s, carry):
        u = vel[s, 0].astype(F32)
        v = vel[s, 1].astype(F32)
        w = vel[s, 2].astype(F32)
        place(buf, s, ramp(w, 1, ycs) - ramp(v, 2, zcs))
        rest[0, s] = ramp(u, 2, zcs)
        rest[1, s] = ramp(u, 1, ycs)
        return carry

    lax.fori_loop(0, 32, one, 0, unroll=2)
    emit(buf, out, 32)


def outer_kernel(vel, lo, hi, rest, out, buf):
    def one(s, carry):
        v = vel[s, 1].astype(F32)
        w = vel[s, 2].astype(F32)
        dxv = along_x([lo[s, 0].astype(F32), v, hi[s, 0].astype(F32)])
        dxw = along_x([lo[s, 1].astype(F32), w, hi[s, 1].astype(F32)])
        place(buf, s, rest[0, s] - dxw)
        place(buf, 32 + s, dxv - rest[1, s])
        return carry

    lax.fori_loop(0, 32, one, 0, unroll=4)
    emit(buf, out, 64)


def inner(vel):
    return pl.pallas_call(
        inner_kernel,
        out_shape=(jax.ShapeDtypeStruct((8, 32, 640), BF16), jax.ShapeDtypeStruct((2, 32, 5, 8, 128), F32)),
        in_specs=[VM],
        out_specs=(VM, VM),
        scratch_shapes=[pltpu.VMEM((32 * 40, 128), F32)],
        compiler_params=pltpu.CompilerParams(vmem_limit_bytes=16 << 20),
        cost_estimate=pl.CostEstimate(flops=10_000_000, bytes_accessed=12_000_000, transcendentals=0),
    )(vel)


def outer(vel, lo, hi, rest):
    return pl.pallas_call(
        outer_kernel,
        out_shape=jax.ShapeDtypeStruct((8, 64, 640), BF16),
        in_specs=[VM] * 4,
        out_specs=VM,
        scratch_shapes=[pltpu.VMEM((64 * 40, 128), F32)],
        compiler_params=pltpu.CompilerParams(vmem_limit_bytes=16 << 20),
        cost_estimate=pl.CostEstimate(flops=10_000_000, bytes_accessed=6_000_000, transcendentals=0),
    )(vel, lo, hi, rest)


def block(K, J):
    return K * NB - K * (K - 1) // 2 + (J - K)


def gram_kernel(one, two, m_out, out, buf, m, sem):
    for j in range(5):
        cols = slice(j * 128, j * 128 + 128)
        for d in range(8):
            buf[j, pl.ds(96 * d, 32, stride=3), :] = one[d, :, cols].astype(F32)
            buf[j, pl.ds(96 * d + 1, 32, stride=3), :] = two[d, 0:32, cols].astype(F32)
            buf[j, pl.ds(96 * d + 2, 32, stride=3), :] = two[d, 32:64, cols].astype(F32)
        m[:, cols] = buf[j].astype(BF16)
    copy = pltpu.make_async_copy(m, m_out, sem)
    copy.start()
    for K in range(NB):
        rows = m[K * S : K * S + S, :]
        res = lax.dot_general(rows, m[K * S :, :], (((1,), (1,)), ((), ())), preferred_element_type=F32)
        for J in range(K, NB):
            b = block(K, J)
            out[b * S : b * S + S, :] = res[:, (J - K) * S : (J - K + 1) * S]
    out[21 * S :, :] = jnp.zeros((S, S), F32)
    copy.wait()


def gram_blocks(one, two):
    return pl.pallas_call(
        gram_kernel,
        out_shape=(jax.ShapeDtypeStruct((NB * S, 640), BF16), jax.ShapeDtypeStruct((22 * S, S), F32)),
        in_specs=[VM, VM],
        out_specs=(HBM, VM),
        scratch_shapes=[
            pltpu.VMEM((5, NB * S, 128), F32),
            pltpu.VMEM((NB * S, 640), BF16),
            pltpu.SemaphoreType.DMA(()),
        ],
        compiler_params=pltpu.CompilerParams(vmem_limit_bytes=32 << 20),
    )(one, two)


SWAP = [(0, 1), (1, 0)]


def scatter_core(v):
    i = lax.axis_index("c")
    h = v.shape[0] // 2
    send = lax.dynamic_slice_in_dim(v, (1 - i) * h, h, 0)
    keep = lax.dynamic_slice_in_dim(v, i * h, h, 0)
    return keep + lax.ppermute(send, "c", SWAP)


def gather_core(v):
    i = lax.axis_index("c")
    h = v.shape[0]
    o = lax.ppermute(v, "c", SWAP)
    out = lax.dynamic_update_slice_in_dim(jnp.zeros((2 * h,) + v.shape[1:], v.dtype), v, i * h, 0)
    return lax.dynamic_update_slice_in_dim(out, o, (1 - i) * h, 0)


def ring(n, k):
    return [(j, (j + k) % n) for j in range(n)]


def scatter_x(v):
    i = lax.axis_index("x")
    h = v.shape[0] // 4
    total = lax.dynamic_slice_in_dim(v, i * h, h, 0)
    got = []
    for k in (2, 1, 3):
        send = lax.dynamic_slice_in_dim(v, ((i + k) % 4) * h, h, 0)
        got.append(lax.ppermute(send, "x", ring(4, k)))
    for g in got:
        total = total + g
    return total


def gather_x(v):
    i = lax.axis_index("x")
    h = v.shape[0]
    parts = {0: v}
    for k in (2, 1, 3):
        parts[k] = lax.ppermute(v, "x", ring(4, k))
    out = jnp.zeros((4 * h,) + v.shape[1:], v.dtype)
    for k in range(4):
        out = lax.dynamic_update_slice_in_dim(out, parts[k], ((i - k) % 4) * h, 0)
    return out


def scatter_yz(v):
    got = lax.all_to_all(v.reshape(32, -1, v.shape[1]), ("y", "z"), 0, 0, tiled=True)
    return got.sum(0)


def gather_yz(v):
    got = lax.all_to_all(jnp.broadcast_to(v[None], (32,) + v.shape), ("y", "z"), 0, 0, tiled=True)
    return got.reshape(-1, v.shape[1])


def total_of(v):
    share = scatter_yz(scatter_x(scatter_core(v))) / POINTS
    return gather_core(gather_x(gather_yz(share)))


BF=jnp.bfloat16
def parts(x):
    a=x.astype(BF); r=x-a.astype(jnp.float32)
    b=r.astype(BF); r=r-b.astype(jnp.float32)
    return a,b,r.astype(BF)
def left(p): a,b,c=p; return jnp.concatenate([a,a,b,a,b,c],axis=1)
def right(p): a,b,c=p; return jnp.concatenate([a,b,a,c,b,a],axis=0)
def mm(l,r): return lax.dot_general(l,r,(((1,),(0,)),((),())),preferred_element_type=jnp.float32)

def bi(K,J): return K*NB-K*(K-1)//2+(J-K)
def lane(v,i): return jnp.broadcast_to(v[:,i:i+1],(8,128))
def sub(v,i): return jnp.broadcast_to(v[i:i+1,:],(8,128))
NV=4
def diag(D,T,ones,fill):
    rows=lax.broadcasted_iota(jnp.int32,(8,128),0)
    lanes=lax.broadcasted_iota(jnp.int32,(8,128),1)
    one=ones[...]
    for g in range(16):
        T[8*g:8*g+8,:]=(rows+8*g==lanes).astype(jnp.float32)
    total=len(fill)
    for g in range(16):
        while fill and total-len(fill)<total*(g+1)//15:
            fill.pop(0)()
        Dg=D[8*g:8*g+8,:]; Wg=T[8*g:8*g+8,:]
        B=[lane(Dg,8*g+m)*one for m in range(8)]
        d={(i,m):sub(B[m],i) for m in range(8) for i in range(m,8)}
        inv=[None]*8; F=[None]*8
        dm={}
        for s in range(8):
            inv[s]=1.0/d[s,s]
            for i in range(s+1,8): dm[i,s]=d[i,s]
            F[s]=jnp.where(rows>s,B[s]*inv[s],0.0)
            for m in range(s+1,8):
                B[m]=B[m]-F[s]*d[m,s]
                for i in range(m,8):
                    d[i,m]=d[i,m]-(d[i,s]*d[m,s])*inv[s]
        piv=d[7,7]
        for s in range(7): piv=jnp.where(rows==s,d[s,s],piv)
        rsq=lax.rsqrt(piv)
        U=[];V=[]
        for s in range(8):
            u=sub(Dg,s); v=sub(Wg,s); U.append(u); V.append(v)
            Dg=Dg-F[s]*u; Wg=Wg-F[s]*v
        Rg=jnp.where(lanes>=rows+8*g,Dg*rsq,0.0); Tg=Wg*rsq
        D[8*g:8*g+8,:]=Rg
        T[8*g:8*g+8,:]=Tg
        r0=8*(g+1+NV)
        if r0<128:
            p=[q.astype(jnp.float32) for q in parts(jnp.concatenate([Rg,Tg],axis=1))]
            rr=jnp.concatenate([p[0],p[1],p[0],p[2],p[1],p[0]],axis=0).astype(BF)
            ll=jnp.concatenate([p[i][:,:128] for i in (0,0,1,0,1,2)],axis=0)
            upd=mm(jnp.transpose(ll)[r0:,:].astype(BF),rr)
            D[r0:,:]=D[r0:,:]-upd[:,:128]
            T[r0:,:]=T[r0:,:]-upd[:,128:]
        for h in range(g+1,min(g+1+NV,16)):
            Dh=D[8*h:8*h+8,:]; Wh=T[8*h:8*h+8,:]
            Bh=[lane(Dh,8*g+m) for m in range(8)]
            for s in range(8):
                f=Bh[s]*inv[s]
                for m in range(s+1,8): Bh[m]=Bh[m]-f*dm[m,s]
                Dh=Dh-f*U[s]; Wh=Wh-f*V[s]
            D[8*h:8*h+8,:]=Dh; T[8*h:8*h+8,:]=Wh
def chol_kernel(a_ref,m_hbm,ones,f_ref,x_ref,A,T,M,TP,RT,RP,XP,m_ref,sem):
    bring=pltpu.make_async_copy(m_hbm,m_ref,sem)
    bring.start()
    def zero():
        for K in range(NB):
            if K: f_ref[K*S:K*S+S,0:K*S]=jnp.zeros((S,K*S),jnp.float32)
    fill=[]
    def put(ref,p):
        for i in range(3): ref[i]=p[i]
    def get(ref): return ref[0],ref[1],ref[2]
    for K in range(NB):
        Dk=A.at[bi(K,K)]
        if K==0:
            Dk[...]=a_ref[0]
        diag(Dk,T,ones,fill)
        if K==0: bring.wait()
        f_ref[K*S:K*S+S,K*S:K*S+S]=Dk[...]
        put(TP,parts(T[...]))
        src=a_ref if K==0 else A
        def panel(J,K=K,src=src):
            r=mm(left(get(TP)),right(parts(src[bi(K,J)])))
            f_ref[K*S:K*S+S,J*S:J*S+S]=r
            put(RT.at[J],parts(jnp.transpose(r))); put(RP.at[J],parts(r))
        def update(I,J,K=K,src=src):
            b=bi(I,J)
            A[b]=src[b]-mm(left(get(RT.at[I])),right(get(RP.at[J])))
        def solve(K=K):
            tp=get(TP)
            if K==0:
                m=m_ref[K*S:K*S+S,:]
                xk=mm(jnp.concatenate(tp,axis=1),jnp.concatenate([m,m,m],axis=0))
            else:
                xk=mm(left(tp),right(parts(M[K*S:K*S+S,:])))
            x_ref[K*S:K*S+S,:]=xk.astype(BF)
            if K<NB-1: put(XP,parts(xk))
        def updm(I,K=K):
            m0=m_ref[I*S:I*S+S,:].astype(jnp.float32) if K==0 else M[I*S:I*S+S,:]
            M[I*S:I*S+S,:]=m0-mm(left(get(RT.at[I])),right(get(XP)))
        if K==NB-1:
            solve(); break
        panel(K+1)
        update(K+1,K+1)
        if K==0: fill.append(zero)
        for J in range(K+2,NB): fill.append(lambda J=J,f=panel: f(J))
        fill.append(solve)
        for I in range(K+1,NB):
            for J in range(I,NB):
                if J>K+1: fill.append(lambda I=I,J=J,f=update: f(I,J))
            fill.append(lambda I=I,f=updm: f(I))
def chol_solve(blocks,m):
    n=m.shape[1]
    vm=pl.BlockSpec(memory_space=pltpu.VMEM)
    return pl.pallas_call(chol_kernel,out_shape=(jax.ShapeDtypeStruct((768,768),jnp.float32),jax.ShapeDtypeStruct((768,n),jnp.bfloat16)),
        in_specs=[vm,HBM,vm],out_specs=(vm,vm),
        scratch_shapes=[pltpu.VMEM((21,S,S),jnp.float32),pltpu.VMEM((S,S),jnp.float32),pltpu.VMEM((768,n),jnp.float32),pltpu.VMEM((3,S,S),BF),pltpu.VMEM((NB,3,S,S),BF),pltpu.VMEM((NB,3,S,S),BF),pltpu.VMEM((3,S,n),BF),pltpu.VMEM((768,n),BF),pltpu.SemaphoreType.DMA(())],
        compiler_params=pltpu.CompilerParams(vmem_limit_bytes=40<<20))(blocks,m,jnp.ones((8,128),jnp.float32))


def body(velocity):
    slabs = 32
    forward = [(i, i + 1) for i in range(slabs - 1)]
    backward = [(i + 1, i) for i in range(slabs - 1)]
    lo = lax.ppermute(velocity[:, 1:, 1:5], ("y", "z"), forward)
    hi = lax.ppermute(velocity[:, 1:, 0:4], ("y", "z"), backward)
    share, rest = inner(velocity)
    one = lax.all_to_all(share, ("x", "c"), 0, 0, tiled=True)
    two = lax.all_to_all(outer(velocity, lo, hi, rest), ("x", "c"), 0, 0, tiled=True)
    matrix, blocks = gram_blocks(one, two)
    total = total_of(blocks).reshape(22, S, S)
    factor, modes = chol_solve(total, matrix)
    return modes.reshape(NB * S, 1, 640), factor


def solution(mesh):
    fine = Mesh(mesh.devices.reshape(4, 2, 4, 8), ("x", "c", "y", "z"))
    in_specs = (P(("x", "c"), None, ("y", "z"), None, None),)
    out_specs = (P(None, ("y", "z"), ("x", "c")), P())
    return jax.shard_map(body, mesh=fine, in_specs=in_specs, out_specs=out_specs, check_vma=False)
```

```python
import jax
import jax.numpy as jnp
from jax import lax
from jax.experimental import pallas as pl
from jax.experimental.pallas import tpu as pltpu
from jax.sharding import Mesh, PartitionSpec as P

weights = (4.0 / 5.0, -1.0 / 5.0, 4.0 / 105.0, -1.0 / 280.0)
POINTS = 163840
NB = 6
S = 128
F32 = jnp.float32
BF16 = jnp.bfloat16
VM = pl.BlockSpec(memory_space=pltpu.VMEM)


def ramp(field, axis, coeffs):
    total = None
    for shift, coeff in coeffs:
        term = coeff * pltpu.roll(field, shift, axis)
        total = term if total is None else total + term
    return total


def tables():
    shape = (5, 8, 128)
    y = lax.broadcasted_iota(jnp.int32, shape, 1)
    z = lax.broadcasted_iota(jnp.int32, shape, 2)
    ycs = []
    for r in range(1, 8):
        up = jnp.where(y + r < 8, weights[r - 1] if r <= 4 else 0.0, 0.0)
        down = jnp.where(y + r >= 8, weights[7 - r] if r >= 4 else 0.0, 0.0)
        ycs.append((8 - r, (up - down).astype(F32)))
    zcs = []
    for k in range(1, 5):
        zcs.append((128 - k, jnp.where(z + k < 128, weights[k - 1], 0.0).astype(F32)))
        zcs.append((k, jnp.where(z >= k, -weights[k - 1], 0.0).astype(F32)))
    return ycs, zcs


def along_x(parts):
    planes = jnp.concatenate(parts, axis=0)
    total = None
    for k in range(1, 5):
        term = weights[k - 1] * (planes[4 + k : 9 + k] - planes[4 - k : 9 - k])
        total = term if total is None else total + term
    return total


def emit(buf, out, rows):
    for p in range(40):
        out[p // 5, :, (p % 5) * 128 : (p % 5 + 1) * 128] = buf[pl.ds(p, rows, stride=40), :].astype(BF16)


def place(buf, row, value):
    buf[pl.ds(pl.multiple_of(row * 40, 8), 40), :] = value.reshape(40, 128)


def inner_kernel(vel, out, rest, buf):
    ycs, zcs = tables()

    def one(s, carry):
        u = vel[s, 0].astype(F32)
        v = vel[s, 1].astype(F32)
        w = vel[s, 2].astype(F32)
        place(buf, s, ramp(w, 1, ycs) - ramp(v, 2, zcs))
        rest[0, s] = ramp(u, 2, zcs)
        rest[1, s] = ramp(u, 1, ycs)
        return carry

    lax.fori_loop(0, 32, one, 0, unroll=2)
    emit(buf, out, 32)


def outer_kernel(vel, lo, hi, rest, out, buf):
    def one(s, carry):
        v = vel[s, 1].astype(F32)
        w = vel[s, 2].astype(F32)
        dxv = along_x([lo[s, 0].astype(F32), v, hi[s, 0].astype(F32)])
        dxw = along_x([lo[s, 1].astype(F32), w, hi[s, 1].astype(F32)])
        place(buf, s, rest[0, s] - dxw)
        place(buf, 32 + s, dxv - rest[1, s])
        return carry

    lax.fori_loop(0, 32, one, 0, unroll=4)
    emit(buf, out, 64)


def inner(vel):
    return pl.pallas_call(
        inner_kernel,
        out_shape=(jax.ShapeDtypeStruct((8, 32, 640), BF16), jax.ShapeDtypeStruct((2, 32, 5, 8, 128), F32)),
        in_specs=[VM],
        out_specs=(VM, VM),
        scratch_shapes=[pltpu.VMEM((32 * 40, 128), F32)],
        compiler_params=pltpu.CompilerParams(vmem_limit_bytes=16 << 20),
        cost_estimate=pl.CostEstimate(flops=10_000_000, bytes_accessed=12_000_000, transcendentals=0),
    )(vel)


def outer(vel, lo, hi, rest):
    return pl.pallas_call(
        outer_kernel,
        out_shape=jax.ShapeDtypeStruct((8, 64, 640), BF16),
        in_specs=[VM] * 4,
        out_specs=VM,
        scratch_shapes=[pltpu.VMEM((64 * 40, 128), F32)],
        compiler_params=pltpu.CompilerParams(vmem_limit_bytes=16 << 20),
        cost_estimate=pl.CostEstimate(flops=10_000_000, bytes_accessed=6_000_000, transcendentals=0),
    )(vel, lo, hi, rest)


SHARE = 296


def above(K, J):
    return K * NB - K * (K + 1) // 2 + (J - K - 1)


def weave(one, two, m, buf, js):
    for j in js:
        cols = slice(j * 128, j * 128 + 128)
        for d in range(8):
            buf[j, pl.ds(96 * d, 32, stride=3), :] = one[d, :, cols].astype(F32)
            buf[j, pl.ds(96 * d + 1, 32, stride=3), :] = two[d, 0:32, cols].astype(F32)
            buf[j, pl.ds(96 * d + 2, 32, stride=3), :] = two[d, 32:64, cols].astype(F32)
        m[:, cols] = buf[j].astype(BF16)


def gram_kernel(one, two, out, buf, m):
    weave(one, two, m, buf, range(5))
    r = lax.broadcasted_iota(jnp.int32, (S, S), 0)
    c = lax.broadcasted_iota(jnp.int32, (S, S), 1)
    out[18 * S :, :] = jnp.zeros((8 * SHARE - 18 * S, S), F32)
    even = None
    for K in range(NB):
        rows = m[K * S : K * S + S, :]
        res = lax.dot_general(rows, m[K * S :, :], (((1,), (1,)), ((), ())), preferred_element_type=F32)
        first = res[:, 0:S]
        if K % 2 == 0:
            even = first
        else:
            p = K // 2
            out[(15 + p) * S : (16 + p) * S, :] = jnp.where(r <= c, even, first)
            out[18 * S + p : 18 * S + p + 1, :] = jnp.sum(jnp.where(r == c, first, 0.0), axis=0, keepdims=True)
        for J in range(K + 1, NB):
            b = above(K, J)
            out[b * S : b * S + S, :] = res[:, (J - K) * S : (J - K + 1) * S]


def gram_blocks(one, two):
    return pl.pallas_call(
        gram_kernel,
        out_shape=jax.ShapeDtypeStruct((8 * SHARE, S), F32),
        in_specs=[VM, VM],
        out_specs=VM,
        scratch_shapes=[
            pltpu.VMEM((5, NB * S, 128), F32),
            pltpu.VMEM((NB * S, 640), BF16),
        ],
        compiler_params=pltpu.CompilerParams(vmem_limit_bytes=32 << 20),
    )(one, two)


SWAP = [(0, 1), (1, 0)]


def scatter_core(v):
    i = lax.axis_index("c")
    h = v.shape[0] // 2
    send = lax.dynamic_slice_in_dim(v, (1 - i) * h, h, 0)
    keep = lax.dynamic_slice_in_dim(v, i * h, h, 0)
    return keep + lax.ppermute(send, "c", SWAP)


def gather_core(v):
    i = lax.axis_index("c")
    h = v.shape[0]
    o = lax.ppermute(v, "c", SWAP)
    out = lax.dynamic_update_slice_in_dim(jnp.zeros((2 * h,) + v.shape[1:], v.dtype), v, i * h, 0)
    return lax.dynamic_update_slice_in_dim(out, o, (1 - i) * h, 0)


def ring(n, k):
    return [(j, (j + k) % n) for j in range(n)]


def scatter_x(v):
    i = lax.axis_index("x")
    h = v.shape[0] // 4
    total = lax.dynamic_slice_in_dim(v, i * h, h, 0)
    got = []
    for k in (2, 1, 3):
        send = lax.dynamic_slice_in_dim(v, ((i + k) % 4) * h, h, 0)
        got.append(lax.ppermute(send, "x", ring(4, k)))
    for g in got:
        total = total + g
    return total


def gather_x(v):
    i = lax.axis_index("x")
    h = v.shape[0]
    parts = {0: v}
    for k in (2, 1, 3):
        parts[k] = lax.ppermute(v, "x", ring(4, k))
    out = jnp.zeros((4 * h,) + v.shape[1:], v.dtype)
    for k in range(4):
        out = lax.dynamic_update_slice_in_dim(out, parts[k], ((i - k) % 4) * h, 0)
    return out


def scatter_yz(v):
    v = jnp.pad(v, ((0, 320 - SHARE), (0, 0)))
    got = lax.all_to_all(v.reshape(32, -1, v.shape[1]), ("y", "z"), 0, 0, tiled=True)
    return got.sum(0)


def gather_yz(v):
    got = lax.all_to_all(jnp.broadcast_to(v[None], (32,) + v.shape), ("y", "z"), 0, 0, tiled=True)
    return got.reshape(-1, v.shape[1])[:SHARE]


def total_of(v):
    share = scatter_yz(scatter_x(scatter_core(v))) / POINTS
    return gather_core(gather_x(gather_yz(share)))


BF=jnp.bfloat16
def parts(x):
    a=x.astype(BF); r=x-a.astype(jnp.float32)
    b=r.astype(BF); r=r-b.astype(jnp.float32)
    return a,b,r.astype(BF)
def left(p): a,b,c=p; return jnp.concatenate([a,a,b,a,b,c],axis=1)
def right(p): a,b,c=p; return jnp.concatenate([a,b,a,c,b,a],axis=0)
def mm(l,r): return lax.dot_general(l,r,(((1,),(0,)),((),())),preferred_element_type=jnp.float32)

def bi(K,J): return K*NB-K*(K-1)//2+(J-K)
def lane(v,i): return jnp.broadcast_to(v[:,i:i+1],(8,128))
def sub(v,i): return jnp.broadcast_to(v[i:i+1,:],(8,128))
NV=4
def diag(D,T,ones,fill):
    rows=lax.broadcasted_iota(jnp.int32,(8,128),0)
    lanes=lax.broadcasted_iota(jnp.int32,(8,128),1)
    one=ones[...]
    for g in range(16):
        T[8*g:8*g+8,:]=(rows+8*g==lanes).astype(jnp.float32)
    total=len(fill)
    for g in range(16):
        while fill and total-len(fill)<total*(g+1)//15:
            fill.pop(0)()
        Dg=D[8*g:8*g+8,:]; Wg=T[8*g:8*g+8,:]
        B=[lane(Dg,8*g+m)*one for m in range(8)]
        d={(i,m):sub(B[m],i) for m in range(8) for i in range(m,8)}
        inv=[None]*8; F=[None]*8
        dm={}
        for s in range(8):
            inv[s]=1.0/d[s,s]
            for i in range(s+1,8): dm[i,s]=d[i,s]
            F[s]=jnp.where(rows>s,B[s]*inv[s],0.0)
            for m in range(s+1,8):
                B[m]=B[m]-F[s]*d[m,s]
                for i in range(m,8):
                    d[i,m]=d[i,m]-(d[i,s]*d[m,s])*inv[s]
        piv=d[7,7]
        for s in range(7): piv=jnp.where(rows==s,d[s,s],piv)
        rsq=lax.rsqrt(piv)
        U=[];V=[]
        for s in range(8):
            u=sub(Dg,s); v=sub(Wg,s); U.append(u); V.append(v)
            Dg=Dg-F[s]*u; Wg=Wg-F[s]*v
        Rg=jnp.where(lanes>=rows+8*g,Dg*rsq,0.0); Tg=Wg*rsq
        D[8*g:8*g+8,:]=Rg
        T[8*g:8*g+8,:]=Tg
        r0=8*(g+1+NV)
        if r0<128:
            p=[q.astype(jnp.float32) for q in parts(jnp.concatenate([Rg,Tg],axis=1))]
            rr=jnp.concatenate([p[0],p[1],p[0],p[2],p[1],p[0]],axis=0).astype(BF)
            ll=jnp.concatenate([p[i][:,:128] for i in (0,0,1,0,1,2)],axis=0)
            upd=mm(jnp.transpose(ll)[r0:,:].astype(BF),rr)
            D[r0:,:]=D[r0:,:]-upd[:,:128]
            T[r0:,:]=T[r0:,:]-upd[:,128:]
        for h in range(g+1,min(g+1+NV,16)):
            Dh=D[8*h:8*h+8,:]; Wh=T[8*h:8*h+8,:]
            Bh=[lane(Dh,8*g+m) for m in range(8)]
            for s in range(8):
                f=Bh[s]*inv[s]
                for m in range(s+1,8): Bh[m]=Bh[m]-f*dm[m,s]
                Dh=Dh-f*U[s]; Wh=Wh-f*V[s]
            D[8*h:8*h+8,:]=Dh; T[8*h:8*h+8,:]=Wh
def chol_kernel(a_ref,one,two,ones,f_out,x_out,A,T,M,TP,RT,RP,XP,m_ref,wb,f_ref,x_ref,sems):
    top=slice(0,4*S); low=slice(4*S,NB*S)
    outs=[pltpu.make_async_copy(v.at[r],o.at[r],sems.at[i]) for i,(v,o,r) in enumerate(((f_ref,f_out,top),(x_ref,x_out,top),(f_ref,f_out,low),(x_ref,x_out,low)))]
    def zero():
        for K in range(NB):
            if K: f_ref[K*S:K*S+S,0:K*S]=jnp.zeros((S,K*S),jnp.float32)
    r_=lax.broadcasted_iota(jnp.int32,(S,S),0); c_=lax.broadcasted_iota(jnp.int32,(S,S),1)
    def tile(b): return a_ref[b*S:b*S+S,:]
    def unpack(p,ks):
        t=tile(15+p); u=jnp.transpose(t)
        if 0 in ks: A[bi(2*p,2*p)]=jnp.where(r_<=c_,t,u)
        if 1 in ks:
            v=jnp.where(r_>c_,t,u)
            A[bi(2*p+1,2*p+1)]=jnp.where(r_==c_,a_ref[18*S+p:18*S+p+1,:],v)
    def base(K,I,J):
        return tile(above(I,J)) if K==0 and I!=J else A[bi(I,J)]
    unpack(0,(0,1))
    fill=[lambda p=p: unpack(p,(0,1)) for p in (1,2)]+[lambda j=j: weave(one,two,m_ref,wb,[j]) for j in range(5)]
    def put(ref,p):
        for i in range(3): ref[i]=p[i]
    def get(ref): return ref[0],ref[1],ref[2]
    for K in range(NB):
        Dk=A.at[bi(K,K)]
        diag(Dk,T,ones,fill)
        if K==4:
            outs[0].start(); outs[1].start()
        f_ref[K*S:K*S+S,K*S:K*S+S]=Dk[...]
        put(TP,parts(T[...]))
        def panel(J,K=K):
            r=mm(left(get(TP)),right(parts(base(K,K,J))))
            f_ref[K*S:K*S+S,J*S:J*S+S]=r
            put(RT.at[J],parts(jnp.transpose(r))); put(RP.at[J],parts(r))
        def update(I,J,K=K):
            b=bi(I,J)
            A[b]=base(K,I,J)-mm(left(get(RT.at[I])),right(get(RP.at[J])))
        def solve(K=K):
            tp=get(TP)
            if K==0:
                m=m_ref[K*S:K*S+S,:]
                xk=mm(jnp.concatenate(tp,axis=1),jnp.concatenate([m,m,m],axis=0))
            else:
                xk=mm(left(tp),right(parts(M[K*S:K*S+S,:])))
            x_ref[K*S:K*S+S,:]=xk.astype(BF)
            if K<NB-1: put(XP,parts(xk))
        def updm(I,K=K):
            m0=m_ref[I*S:I*S+S,:].astype(jnp.float32) if K==0 else M[I*S:I*S+S,:]
            M[I*S:I*S+S,:]=m0-mm(left(get(RT.at[I])),right(get(XP)))
        if K==NB-1:
            solve()
            outs[2].start(); outs[3].start()
            for o in outs: o.wait()
            break
        panel(K+1)
        update(K+1,K+1)
        if K==0: fill.append(zero)
        for J in range(K+2,NB): fill.append(lambda J=J,f=panel: f(J))
        fill.append(solve)
        for I in range(K+1,NB):
            for J in range(I,NB):
                if J>K+1: fill.append(lambda I=I,J=J,f=update: f(I,J))
            fill.append(lambda I=I,f=updm: f(I))
def chol_solve(blocks,one,two):
    n=one.shape[2]
    vm=pl.BlockSpec(memory_space=pltpu.VMEM)
    return pl.pallas_call(chol_kernel,out_shape=(jax.ShapeDtypeStruct((768,768),jnp.float32),jax.ShapeDtypeStruct((768,n),jnp.bfloat16)),
        in_specs=[vm,vm,vm,vm],out_specs=(pl.BlockSpec(memory_space=pl.ANY),pl.BlockSpec(memory_space=pl.ANY)),
        scratch_shapes=[pltpu.VMEM((21,S,S),jnp.float32),pltpu.VMEM((S,S),jnp.float32),pltpu.VMEM((768,n),jnp.float32),pltpu.VMEM((3,S,S),BF),pltpu.VMEM((NB,3,S,S),BF),pltpu.VMEM((NB,3,S,S),BF),pltpu.VMEM((3,S,n),BF),pltpu.VMEM((768,n),BF),pltpu.VMEM((5,768,128),jnp.float32),pltpu.VMEM((768,768),jnp.float32),pltpu.VMEM((768,n),BF),pltpu.SemaphoreType.DMA((4,))],
        compiler_params=pltpu.CompilerParams(vmem_limit_bytes=40<<20))(blocks,one,two,jnp.ones((8,128),jnp.float32))


def body(velocity):
    slabs = 32
    forward = [(i, i + 1) for i in range(slabs - 1)]
    backward = [(i + 1, i) for i in range(slabs - 1)]
    lo = lax.ppermute(velocity[:, 1:, 1:5], ("y", "z"), forward)
    hi = lax.ppermute(velocity[:, 1:, 0:4], ("y", "z"), backward)
    share, rest = inner(velocity)
    one = lax.all_to_all(share, ("x", "c"), 0, 0, tiled=True)
    two = lax.all_to_all(outer(velocity, lo, hi, rest), ("x", "c"), 0, 0, tiled=True)
    total = total_of(gram_blocks(one, two))
    factor, modes = chol_solve(total, one, two)
    return modes.reshape(NB * S, 1, 640), factor


def solution(mesh):
    fine = Mesh(mesh.devices.reshape(4, 2, 4, 8), ("x", "c", "y", "z"))
    in_specs = (P(("x", "c"), None, ("y", "z"), None, None),)
    out_specs = (P(None, ("y", "z"), ("x", "c")), P())
    return jax.shard_map(body, mesh=fine, in_specs=in_specs, out_specs=out_specs, check_vma=False)
```

```python
import jax
import jax.numpy as jnp
from jax import lax
from jax.experimental import pallas as pl
from jax.experimental.pallas import tpu as pltpu
from jax.sharding import Mesh, PartitionSpec as P

weights = (4.0 / 5.0, -1.0 / 5.0, 4.0 / 105.0, -1.0 / 280.0)
POINTS = 163840
NB = 6
S = 128
F32 = jnp.float32
BF16 = jnp.bfloat16
VM = pl.BlockSpec(memory_space=pltpu.VMEM)


def ramp(field, axis, coeffs):
    total = None
    for shift, coeff in coeffs:
        term = coeff * pltpu.roll(field, shift, axis)
        total = term if total is None else total + term
    return total


def tables():
    shape = (5, 8, 128)
    y = lax.broadcasted_iota(jnp.int32, shape, 1)
    z = lax.broadcasted_iota(jnp.int32, shape, 2)
    ycs = []
    for r in range(1, 8):
        up = jnp.where(y + r < 8, weights[r - 1] if r <= 4 else 0.0, 0.0)
        down = jnp.where(y + r >= 8, weights[7 - r] if r >= 4 else 0.0, 0.0)
        ycs.append((8 - r, (up - down).astype(F32)))
    zcs = []
    for k in range(1, 5):
        zcs.append((128 - k, jnp.where(z + k < 128, weights[k - 1], 0.0).astype(F32)))
        zcs.append((k, jnp.where(z >= k, -weights[k - 1], 0.0).astype(F32)))
    return ycs, zcs


def along_x(parts):
    planes = jnp.concatenate(parts, axis=0)
    total = None
    for k in range(1, 5):
        term = weights[k - 1] * (planes[4 + k : 9 + k] - planes[4 - k : 9 - k])
        total = term if total is None else total + term
    return total


def emit(buf, out, rows):
    for p in range(40):
        out[p // 5, :, (p % 5) * 128 : (p % 5 + 1) * 128] = buf[pl.ds(p, rows, stride=40), :].astype(BF16)


def place(buf, row, value):
    buf[pl.ds(pl.multiple_of(row * 40, 8), 40), :] = value.reshape(40, 128)


def inner_kernel(vel, out, rest, buf):
    ycs, zcs = tables()

    def one(s, carry):
        u = vel[s, 0].astype(F32)
        v = vel[s, 1].astype(F32)
        w = vel[s, 2].astype(F32)
        place(buf, s, ramp(w, 1, ycs) - ramp(v, 2, zcs))
        rest[0, s] = ramp(u, 2, zcs)
        rest[1, s] = ramp(u, 1, ycs)
        return carry

    lax.fori_loop(0, 32, one, 0, unroll=2)
    emit(buf, out, 32)


def outer_kernel(vel, lo, hi, rest, out, buf):
    def one(s, carry):
        v = vel[s, 1].astype(F32)
        w = vel[s, 2].astype(F32)
        dxv = along_x([lo[s, 0].astype(F32), v, hi[s, 0].astype(F32)])
        dxw = along_x([lo[s, 1].astype(F32), w, hi[s, 1].astype(F32)])
        place(buf, s, rest[0, s] - dxw)
        place(buf, 32 + s, dxv - rest[1, s])
        return carry

    lax.fori_loop(0, 32, one, 0, unroll=4)
    emit(buf, out, 64)


def inner(vel):
    return pl.pallas_call(
        inner_kernel,
        out_shape=(jax.ShapeDtypeStruct((8, 32, 640), BF16), jax.ShapeDtypeStruct((2, 32, 5, 8, 128), F32)),
        in_specs=[VM],
        out_specs=(VM, VM),
        scratch_shapes=[pltpu.VMEM((32 * 40, 128), F32)],
        compiler_params=pltpu.CompilerParams(vmem_limit_bytes=16 << 20),
        cost_estimate=pl.CostEstimate(flops=10_000_000, bytes_accessed=12_000_000, transcendentals=0),
    )(vel)


def outer(vel, lo, hi, rest):
    return pl.pallas_call(
        outer_kernel,
        out_shape=jax.ShapeDtypeStruct((8, 64, 640), BF16),
        in_specs=[VM] * 4,
        out_specs=VM,
        scratch_shapes=[pltpu.VMEM((64 * 40, 128), F32)],
        compiler_params=pltpu.CompilerParams(vmem_limit_bytes=16 << 20),
        cost_estimate=pl.CostEstimate(flops=10_000_000, bytes_accessed=6_000_000, transcendentals=0),
    )(vel, lo, hi, rest)


SHARE = 296


def above(K, J):
    return K * NB - K * (K + 1) // 2 + (J - K - 1)


def weave(one, two, m, buf, js):
    for j in js:
        cols = slice(j * 128, j * 128 + 128)
        for d in range(8):
            buf[j, pl.ds(96 * d, 32, stride=3), :] = one[d, :, cols].astype(F32)
            buf[j, pl.ds(96 * d + 1, 32, stride=3), :] = two[d, 0:32, cols].astype(F32)
            buf[j, pl.ds(96 * d + 2, 32, stride=3), :] = two[d, 32:64, cols].astype(F32)
        m[:, cols] = buf[j].astype(BF16)


def gram_kernel(one, two, out, buf, m):
    weave(one, two, m, buf, range(5))
    r = lax.broadcasted_iota(jnp.int32, (S, S), 0)
    c = lax.broadcasted_iota(jnp.int32, (S, S), 1)
    out[18 * S :, :] = jnp.zeros((8 * SHARE - 18 * S, S), F32)
    even = None
    for K in range(NB):
        rows = m[K * S : K * S + S, :]
        res = lax.dot_general(rows, m[K * S :, :], (((1,), (1,)), ((), ())), preferred_element_type=F32)
        first = res[:, 0:S]
        if K % 2 == 0:
            even = first
        else:
            p = K // 2
            out[(15 + p) * S : (16 + p) * S, :] = jnp.where(r <= c, even, first)
            out[18 * S + p : 18 * S + p + 1, :] = jnp.sum(jnp.where(r == c, first, 0.0), axis=0, keepdims=True)
        for J in range(K + 1, NB):
            b = above(K, J)
            out[b * S : b * S + S, :] = res[:, (J - K) * S : (J - K + 1) * S]


def gram_blocks(one, two):
    return pl.pallas_call(
        gram_kernel,
        out_shape=jax.ShapeDtypeStruct((8 * SHARE, S), F32),
        in_specs=[VM, VM],
        out_specs=VM,
        scratch_shapes=[
            pltpu.VMEM((5, NB * S, 128), F32),
            pltpu.VMEM((NB * S, 640), BF16),
        ],
        compiler_params=pltpu.CompilerParams(vmem_limit_bytes=32 << 20),
    )(one, two)


SWAP = [(0, 1), (1, 0)]


def scatter_core(v):
    i = lax.axis_index("c")
    h = v.shape[0] // 2
    send = lax.dynamic_slice_in_dim(v, (1 - i) * h, h, 0)
    keep = lax.dynamic_slice_in_dim(v, i * h, h, 0)
    return keep + lax.ppermute(send, "c", SWAP)


def gather_core(v):
    i = lax.axis_index("c")
    h = v.shape[0]
    o = lax.ppermute(v, "c", SWAP)
    out = lax.dynamic_update_slice_in_dim(jnp.zeros((2 * h,) + v.shape[1:], v.dtype), v, i * h, 0)
    return lax.dynamic_update_slice_in_dim(out, o, (1 - i) * h, 0)


def ring(n, k):
    return [(j, (j + k) % n) for j in range(n)]


def scatter_ring(v, axis):
    i = lax.axis_index(axis)
    h = v.shape[0] // 4
    total = lax.dynamic_slice_in_dim(v, i * h, h, 0)
    got = []
    for k in (2, 1, 3):
        send = lax.dynamic_slice_in_dim(v, ((i + k) % 4) * h, h, 0)
        got.append(lax.ppermute(send, axis, ring(4, k)))
    for g in got:
        total = total + g
    return total


def gather_ring(v, axis):
    i = lax.axis_index(axis)
    h = v.shape[0]
    parts = {0: v}
    for k in (2, 1, 3):
        parts[k] = lax.ppermute(v, axis, ring(4, k))
    out = jnp.zeros((4 * h,) + v.shape[1:], v.dtype)
    for k in range(4):
        out = lax.dynamic_update_slice_in_dim(out, parts[k], ((i - k) % 4) * h, 0)
    return out


def scatter_z(v):
    return lax.all_to_all(v.reshape(8, -1, v.shape[1]), "z", 0, 0, tiled=True).sum(0)


def gather_z(v):
    got = lax.all_to_all(jnp.broadcast_to(v[None], (8,) + v.shape), "z", 0, 0, tiled=True)
    return got.reshape(-1, v.shape[1])


def total_of(v):
    share = scatter_ring(scatter_core(v), "x")
    share = scatter_ring(jnp.pad(share, ((0, 320 - SHARE), (0, 0))), "y")
    share = lax.all_to_all(jnp.broadcast_to(share[None], (8,) + share.shape), "z", 0, 0, tiled=True).sum(0) / POINTS
    return gather_core(gather_ring(gather_ring(share, "y")[:SHARE], "x"))


BF=jnp.bfloat16
def parts(x):
    a=x.astype(BF); r=x-a.astype(jnp.float32)
    b=r.astype(BF); r=r-b.astype(jnp.float32)
    return a,b,r.astype(BF)
def left(p): a,b,c=p; return jnp.concatenate([a,a,b,a,b,c],axis=1)
def right(p): a,b,c=p; return jnp.concatenate([a,b,a,c,b,a],axis=0)
def mm(l,r): return lax.dot_general(l,r,(((1,),(0,)),((),())),preferred_element_type=jnp.float32)

def bi(K,J): return K*NB-K*(K-1)//2+(J-K)
def lane(v,i): return jnp.broadcast_to(v[:,i:i+1],(8,128))
def sub(v,i): return jnp.broadcast_to(v[i:i+1,:],(8,128))
NV=4
def diag(D,T,ones,fill):
    rows=lax.broadcasted_iota(jnp.int32,(8,128),0)
    lanes=lax.broadcasted_iota(jnp.int32,(8,128),1)
    one=ones[...]
    for g in range(16):
        T[8*g:8*g+8,:]=(rows+8*g==lanes).astype(jnp.float32)
    total=len(fill)
    for g in range(16):
        while fill and total-len(fill)<total*(g+1)//15:
            fill.pop(0)()
        Dg=D[8*g:8*g+8,:]; Wg=T[8*g:8*g+8,:]
        B=[lane(Dg,8*g+m)*one for m in range(8)]
        d={(i,m):sub(B[m],i) for m in range(8) for i in range(m,8)}
        inv=[None]*8; F=[None]*8
        dm={}
        for s in range(8):
            inv[s]=1.0/d[s,s]
            for i in range(s+1,8): dm[i,s]=d[i,s]
            F[s]=jnp.where(rows>s,B[s]*inv[s],0.0)
            for m in range(s+1,8):
                B[m]=B[m]-F[s]*d[m,s]
                for i in range(m,8):
                    d[i,m]=d[i,m]-(d[i,s]*d[m,s])*inv[s]
        piv=d[7,7]
        for s in range(7): piv=jnp.where(rows==s,d[s,s],piv)
        rsq=lax.rsqrt(piv)
        U=[];V=[]
        for s in range(8):
            u=sub(Dg,s); v=sub(Wg,s); U.append(u); V.append(v)
            Dg=Dg-F[s]*u; Wg=Wg-F[s]*v
        Rg=jnp.where(lanes>=rows+8*g,Dg*rsq,0.0); Tg=Wg*rsq
        D[8*g:8*g+8,:]=Rg
        T[8*g:8*g+8,:]=Tg
        r0=8*(g+1+NV)
        if r0<128:
            p=[q.astype(jnp.float32) for q in parts(jnp.concatenate([Rg,Tg],axis=1))]
            rr=jnp.concatenate([p[0],p[1],p[0],p[2],p[1],p[0]],axis=0).astype(BF)
            ll=jnp.concatenate([p[i][:,:128] for i in (0,0,1,0,1,2)],axis=0)
            upd=mm(jnp.transpose(ll)[r0:,:].astype(BF),rr)
            D[r0:,:]=D[r0:,:]-upd[:,:128]
            T[r0:,:]=T[r0:,:]-upd[:,128:]
        for h in range(g+1,min(g+1+NV,16)):
            Dh=D[8*h:8*h+8,:]; Wh=T[8*h:8*h+8,:]
            Bh=[lane(Dh,8*g+m) for m in range(8)]
            for s in range(8):
                f=Bh[s]*inv[s]
                for m in range(s+1,8): Bh[m]=Bh[m]-f*dm[m,s]
                Dh=Dh-f*U[s]; Wh=Wh-f*V[s]
            D[8*h:8*h+8,:]=Dh; T[8*h:8*h+8,:]=Wh
def chol_kernel(a_ref,one,two,ones,f_out,x_out,A,T,M,TP,RT,RP,XP,m_ref,wb,f_ref,x_ref,sems):
    top=slice(0,4*S); low=slice(4*S,NB*S)
    outs=[pltpu.make_async_copy(v.at[r],o.at[r],sems.at[i]) for i,(v,o,r) in enumerate(((f_ref,f_out,top),(x_ref,x_out,top),(f_ref,f_out,low),(x_ref,x_out,low)))]
    def zero():
        for K in range(NB):
            if K: f_ref[K*S:K*S+S,0:K*S]=jnp.zeros((S,K*S),jnp.float32)
    r_=lax.broadcasted_iota(jnp.int32,(S,S),0); c_=lax.broadcasted_iota(jnp.int32,(S,S),1)
    def tile(b): return a_ref[b*S:b*S+S,:]
    def unpack(p,ks):
        t=tile(15+p); u=jnp.transpose(t)
        if 0 in ks: A[bi(2*p,2*p)]=jnp.where(r_<=c_,t,u)
        if 1 in ks:
            v=jnp.where(r_>c_,t,u)
            A[bi(2*p+1,2*p+1)]=jnp.where(r_==c_,a_ref[18*S+p:18*S+p+1,:],v)
    def base(K,I,J):
        return tile(above(I,J)) if K==0 and I!=J else A[bi(I,J)]
    unpack(0,(0,1))
    fill=[lambda p=p: unpack(p,(0,1)) for p in (1,2)]+[lambda j=j: weave(one,two,m_ref,wb,[j]) for j in range(5)]
    def put(ref,p):
        for i in range(3): ref[i]=p[i]
    def get(ref): return ref[0],ref[1],ref[2]
    for K in range(NB):
        Dk=A.at[bi(K,K)]
        diag(Dk,T,ones,fill)
        if K==4:
            outs[0].start(); outs[1].start()
        f_ref[K*S:K*S+S,K*S:K*S+S]=Dk[...]
        put(TP,parts(T[...]))
        def panel(J,K=K):
            r=mm(left(get(TP)),right(parts(base(K,K,J))))
            f_ref[K*S:K*S+S,J*S:J*S+S]=r
            put(RT.at[J],parts(jnp.transpose(r))); put(RP.at[J],parts(r))
        def update(I,J,K=K):
            b=bi(I,J)
            A[b]=base(K,I,J)-mm(left(get(RT.at[I])),right(get(RP.at[J])))
        def solve(K=K):
            tp=get(TP)
            if K==0:
                m=m_ref[K*S:K*S+S,:]
                xk=mm(jnp.concatenate(tp,axis=1),jnp.concatenate([m,m,m],axis=0))
            else:
                xk=mm(left(tp),right(parts(M[K*S:K*S+S,:])))
            x_ref[K*S:K*S+S,:]=xk.astype(BF)
            if K<NB-1: put(XP,parts(xk))
        def updm(I,K=K):
            m0=m_ref[I*S:I*S+S,:].astype(jnp.float32) if K==0 else M[I*S:I*S+S,:]
            M[I*S:I*S+S,:]=m0-mm(left(get(RT.at[I])),right(get(XP)))
        if K==NB-1:
            solve()
            outs[2].start(); outs[3].start()
            for o in outs: o.wait()
            break
        panel(K+1)
        update(K+1,K+1)
        if K==0: fill.append(zero)
        for J in range(K+2,NB): fill.append(lambda J=J,f=panel: f(J))
        fill.append(solve)
        for I in range(K+1,NB):
            for J in range(I,NB):
                if J>K+1: fill.append(lambda I=I,J=J,f=update: f(I,J))
            fill.append(lambda I=I,f=updm: f(I))
def chol_solve(blocks,one,two):
    n=one.shape[2]
    vm=pl.BlockSpec(memory_space=pltpu.VMEM)
    return pl.pallas_call(chol_kernel,out_shape=(jax.ShapeDtypeStruct((768,768),jnp.float32),jax.ShapeDtypeStruct((768,n),jnp.bfloat16)),
        in_specs=[vm,vm,vm,vm],out_specs=(pl.BlockSpec(memory_space=pl.ANY),pl.BlockSpec(memory_space=pl.ANY)),
        scratch_shapes=[pltpu.VMEM((21,S,S),jnp.float32),pltpu.VMEM((S,S),jnp.float32),pltpu.VMEM((768,n),jnp.float32),pltpu.VMEM((3,S,S),BF),pltpu.VMEM((NB,3,S,S),BF),pltpu.VMEM((NB,3,S,S),BF),pltpu.VMEM((3,S,n),BF),pltpu.VMEM((768,n),BF),pltpu.VMEM((5,768,128),jnp.float32),pltpu.VMEM((768,768),jnp.float32),pltpu.VMEM((768,n),BF),pltpu.SemaphoreType.DMA((4,))],
        compiler_params=pltpu.CompilerParams(vmem_limit_bytes=40<<20))(blocks,one,two,jnp.ones((8,128),jnp.float32))


def body(velocity):
    slabs = 32
    forward = [(i, i + 1) for i in range(slabs - 1)]
    backward = [(i + 1, i) for i in range(slabs - 1)]
    lo = lax.ppermute(velocity[:, 1:, 1:5], ("y", "z"), forward)
    hi = lax.ppermute(velocity[:, 1:, 0:4], ("y", "z"), backward)
    share, rest = inner(velocity)
    one = lax.all_to_all(share, ("x", "c"), 0, 0, tiled=True)
    two = lax.all_to_all(outer(velocity, lo, hi, rest), ("x", "c"), 0, 0, tiled=True)
    total = total_of(gram_blocks(one, two))
    factor, modes = chol_solve(total, one, two)
    return modes.reshape(NB * S, 1, 640), factor


def solution(mesh):
    fine = Mesh(mesh.devices.reshape(4, 2, 4, 8), ("x", "c", "y", "z"))
    in_specs = (P(("x", "c"), None, ("y", "z"), None, None),)
    out_specs = (P(None, ("y", "z"), ("x", "c")), P())
    return jax.shard_map(body, mesh=fine, in_specs=in_specs, out_specs=out_specs, check_vma=False)
```

```python
import jax
import jax.numpy as jnp
from jax import lax
from jax.experimental import pallas as pl
from jax.experimental.pallas import tpu as pltpu
from jax.sharding import Mesh, PartitionSpec as P

weights = (4.0 / 5.0, -1.0 / 5.0, 4.0 / 105.0, -1.0 / 280.0)
POINTS = 163840
NB = 6
S = 128
F32 = jnp.float32
BF16 = jnp.bfloat16
VM = pl.BlockSpec(memory_space=pltpu.VMEM)


def ramp(field, axis, coeffs):
    total = None
    for shift, coeff in coeffs:
        term = coeff * pltpu.roll(field, shift, axis)
        total = term if total is None else total + term
    return total


def tables():
    shape = (5, 8, 128)
    y = lax.broadcasted_iota(jnp.int32, shape, 1)
    z = lax.broadcasted_iota(jnp.int32, shape, 2)
    ycs = []
    for r in range(1, 8):
        up = jnp.where(y + r < 8, weights[r - 1] if r <= 4 else 0.0, 0.0)
        down = jnp.where(y + r >= 8, weights[7 - r] if r >= 4 else 0.0, 0.0)
        ycs.append((8 - r, (up - down).astype(F32)))
    zcs = []
    for k in range(1, 5):
        zcs.append((128 - k, jnp.where(z + k < 128, weights[k - 1], 0.0).astype(F32)))
        zcs.append((k, jnp.where(z >= k, -weights[k - 1], 0.0).astype(F32)))
    return ycs, zcs


def along_x(parts):
    planes = jnp.concatenate(parts, axis=0)
    total = None
    for k in range(1, 5):
        term = weights[k - 1] * (planes[4 + k : 9 + k] - planes[4 - k : 9 - k])
        total = term if total is None else total + term
    return total


def emit(buf, out, rows):
    for p in range(40):
        out[p // 5, :, (p % 5) * 128 : (p % 5 + 1) * 128] = buf[pl.ds(p, rows, stride=40), :].astype(BF16)


def place(buf, row, value):
    buf[pl.ds(pl.multiple_of(row * 40, 8), 40), :] = value.reshape(40, 128)


def inner_kernel(vel, out, rest, buf):
    ycs, zcs = tables()

    def one(s, carry):
        u = vel[s, 0].astype(F32)
        v = vel[s, 1].astype(F32)
        w = vel[s, 2].astype(F32)
        place(buf, s, ramp(w, 1, ycs) - ramp(v, 2, zcs))
        rest[0, s] = ramp(u, 2, zcs)
        rest[1, s] = ramp(u, 1, ycs)
        return carry

    lax.fori_loop(0, 32, one, 0, unroll=2)
    emit(buf, out, 32)


def outer_kernel(vel, lo, hi, rest, out, buf):
    def one(s, carry):
        v = vel[s, 1].astype(F32)
        w = vel[s, 2].astype(F32)
        dxv = along_x([lo[s, 0].astype(F32), v, hi[s, 0].astype(F32)])
        dxw = along_x([lo[s, 1].astype(F32), w, hi[s, 1].astype(F32)])
        place(buf, s, rest[0, s] - dxw)
        place(buf, 32 + s, dxv - rest[1, s])
        return carry

    lax.fori_loop(0, 32, one, 0, unroll=8)
    emit(buf, out, 64)


def inner(vel):
    return pl.pallas_call(
        inner_kernel,
        out_shape=(jax.ShapeDtypeStruct((8, 32, 640), BF16), jax.ShapeDtypeStruct((2, 32, 5, 8, 128), F32)),
        in_specs=[VM],
        out_specs=(VM, VM),
        scratch_shapes=[pltpu.VMEM((32 * 40, 128), F32)],
        compiler_params=pltpu.CompilerParams(vmem_limit_bytes=16 << 20),
        cost_estimate=pl.CostEstimate(flops=10_000_000, bytes_accessed=12_000_000, transcendentals=0),
    )(vel)


def outer(vel, lo, hi, rest):
    return pl.pallas_call(
        outer_kernel,
        out_shape=jax.ShapeDtypeStruct((8, 64, 640), BF16),
        in_specs=[VM] * 4,
        out_specs=VM,
        scratch_shapes=[pltpu.VMEM((64 * 40, 128), F32)],
        compiler_params=pltpu.CompilerParams(vmem_limit_bytes=16 << 20),
        cost_estimate=pl.CostEstimate(flops=10_000_000, bytes_accessed=6_000_000, transcendentals=0),
    )(vel, lo, hi, rest)


SHARE = 296


def above(K, J):
    return K * NB - K * (K + 1) // 2 + (J - K - 1)


def weave(one, two, m, buf, js):
    for j in js:
        cols = slice(j * 128, j * 128 + 128)
        for d in range(8):
            buf[j, pl.ds(96 * d, 32, stride=3), :] = one[d, :, cols].astype(F32)
            buf[j, pl.ds(96 * d + 1, 32, stride=3), :] = two[d, 0:32, cols].astype(F32)
            buf[j, pl.ds(96 * d + 2, 32, stride=3), :] = two[d, 32:64, cols].astype(F32)
        m[:, cols] = buf[j].astype(BF16)


def gram_kernel(one, two, out, buf, m):
    weave(one, two, m, buf, range(5))
    r = lax.broadcasted_iota(jnp.int32, (S, S), 0)
    c = lax.broadcasted_iota(jnp.int32, (S, S), 1)
    out[18 * S :, :] = jnp.zeros((8 * SHARE - 18 * S, S), F32)
    even = None
    for K in range(NB):
        rows = m[K * S : K * S + S, :]
        res = lax.dot_general(rows, m[K * S :, :], (((1,), (1,)), ((), ())), preferred_element_type=F32)
        first = res[:, 0:S]
        if K % 2 == 0:
            even = first
        else:
            p = K // 2
            out[(15 + p) * S : (16 + p) * S, :] = jnp.where(r <= c, even, first)
            out[18 * S + p : 18 * S + p + 1, :] = jnp.sum(jnp.where(r == c, first, 0.0), axis=0, keepdims=True)
        for J in range(K + 1, NB):
            b = above(K, J)
            out[b * S : b * S + S, :] = res[:, (J - K) * S : (J - K + 1) * S]


def gram_blocks(one, two):
    return pl.pallas_call(
        gram_kernel,
        out_shape=jax.ShapeDtypeStruct((8 * SHARE, S), F32),
        in_specs=[VM, VM],
        out_specs=VM,
        scratch_shapes=[
            pltpu.VMEM((5, NB * S, 128), F32),
            pltpu.VMEM((NB * S, 640), BF16),
        ],
        compiler_params=pltpu.CompilerParams(vmem_limit_bytes=32 << 20),
    )(one, two)


SWAP = [(0, 1), (1, 0)]


def scatter_core(v):
    i = lax.axis_index("c")
    h = v.shape[0] // 2
    send = lax.dynamic_slice_in_dim(v, (1 - i) * h, h, 0)
    keep = lax.dynamic_slice_in_dim(v, i * h, h, 0)
    return keep + lax.ppermute(send, "c", SWAP)


def gather_core(v):
    i = lax.axis_index("c")
    h = v.shape[0]
    o = lax.ppermute(v, "c", SWAP)
    out = lax.dynamic_update_slice_in_dim(jnp.zeros((2 * h,) + v.shape[1:], v.dtype), v, i * h, 0)
    return lax.dynamic_update_slice_in_dim(out, o, (1 - i) * h, 0)


def ring(n, k):
    return [(j, (j + k) % n) for j in range(n)]


def scatter_ring(v, axis):
    i = lax.axis_index(axis)
    h = v.shape[0] // 4
    total = lax.dynamic_slice_in_dim(v, i * h, h, 0)
    got = []
    for k in (2, 1, 3):
        send = lax.dynamic_slice_in_dim(v, ((i + k) % 4) * h, h, 0)
        got.append(lax.ppermute(send, axis, ring(4, k)))
    for g in got:
        total = total + g
    return total


def gather_ring(v, axis):
    i = lax.axis_index(axis)
    h = v.shape[0]
    parts = {0: v}
    for k in (2, 1, 3):
        parts[k] = lax.ppermute(v, axis, ring(4, k))
    out = jnp.zeros((4 * h,) + v.shape[1:], v.dtype)
    for k in range(4):
        out = lax.dynamic_update_slice_in_dim(out, parts[k], ((i - k) % 4) * h, 0)
    return out


def scatter_z(v):
    return lax.all_to_all(v.reshape(8, -1, v.shape[1]), "z", 0, 0, tiled=True).sum(0)


def gather_z(v):
    got = lax.all_to_all(jnp.broadcast_to(v[None], (8,) + v.shape), "z", 0, 0, tiled=True)
    return got.reshape(-1, v.shape[1])


def total_of(v):
    share = scatter_ring(scatter_core(v), "x")
    share = scatter_ring(jnp.pad(share, ((0, 320 - SHARE), (0, 0))), "y")
    share = lax.all_to_all(jnp.broadcast_to(share[None], (8,) + share.shape), "z", 0, 0, tiled=True).sum(0) / POINTS
    return gather_core(gather_ring(gather_ring(share, "y")[:SHARE], "x"))


BF=jnp.bfloat16
def parts(x):
    a=x.astype(BF); r=x-a.astype(jnp.float32)
    b=r.astype(BF); r=r-b.astype(jnp.float32)
    return a,b,r.astype(BF)
def left(p): a,b,c=p; return jnp.concatenate([a,a,b,a,b,c],axis=1)
def right(p): a,b,c=p; return jnp.concatenate([a,b,a,c,b,a],axis=0)
def mm(l,r): return lax.dot_general(l,r,(((1,),(0,)),((),())),preferred_element_type=jnp.float32)

def bi(K,J): return K*NB-K*(K-1)//2+(J-K)
def lane(v,i): return jnp.broadcast_to(v[:,i:i+1],(8,128))
def sub(v,i): return jnp.broadcast_to(v[i:i+1,:],(8,128))
NV=4
def diag(D,T,ones,fill):
    rows=lax.broadcasted_iota(jnp.int32,(8,128),0)
    lanes=lax.broadcasted_iota(jnp.int32,(8,128),1)
    one=ones[...]
    for g in range(16):
        T[8*g:8*g+8,:]=(rows+8*g==lanes).astype(jnp.float32)
    total=len(fill)
    for g in range(16):
        while fill and total-len(fill)<total*(g+1)//15:
            fill.pop(0)()
        Dg=D[8*g:8*g+8,:]; Wg=T[8*g:8*g+8,:]
        B=[lane(Dg,8*g+m)*one for m in range(8)]
        d={(i,m):sub(B[m],i) for m in range(8) for i in range(m,8)}
        inv=[None]*8; F=[None]*8
        dm={}
        for s in range(8):
            inv[s]=1.0/d[s,s]
            for i in range(s+1,8): dm[i,s]=d[i,s]
            F[s]=jnp.where(rows>s,B[s]*inv[s],0.0)
            for m in range(s+1,8):
                B[m]=B[m]-F[s]*d[m,s]
                for i in range(m,8):
                    d[i,m]=d[i,m]-(d[i,s]*d[m,s])*inv[s]
        piv=d[7,7]
        for s in range(7): piv=jnp.where(rows==s,d[s,s],piv)
        rsq=lax.rsqrt(piv)
        U=[];V=[]
        for s in range(8):
            u=sub(Dg,s); v=sub(Wg,s); U.append(u); V.append(v)
            Dg=Dg-F[s]*u; Wg=Wg-F[s]*v
        Rg=jnp.where(lanes>=rows+8*g,Dg*rsq,0.0); Tg=Wg*rsq
        D[8*g:8*g+8,:]=Rg
        T[8*g:8*g+8,:]=Tg
        r0=8*(g+1+NV)
        if r0<128:
            p=[q.astype(jnp.float32) for q in parts(jnp.concatenate([Rg,Tg],axis=1))]
            rr=jnp.concatenate([p[0],p[1],p[0],p[2],p[1],p[0]],axis=0).astype(BF)
            ll=jnp.concatenate([p[i][:,:128] for i in (0,0,1,0,1,2)],axis=0)
            upd=mm(jnp.transpose(ll)[r0:,:].astype(BF),rr)
            D[r0:,:]=D[r0:,:]-upd[:,:128]
            T[r0:,:]=T[r0:,:]-upd[:,128:]
        for h in range(g+1,min(g+1+NV,16)):
            Dh=D[8*h:8*h+8,:]; Wh=T[8*h:8*h+8,:]
            Bh=[lane(Dh,8*g+m) for m in range(8)]
            for s in range(8):
                f=Bh[s]*inv[s]
                for m in range(s+1,8): Bh[m]=Bh[m]-f*dm[m,s]
                Dh=Dh-f*U[s]; Wh=Wh-f*V[s]
            D[8*h:8*h+8,:]=Dh; T[8*h:8*h+8,:]=Wh
def chol_kernel(a_ref,one,two,ones,f_out,x_out,A,T,M,TP,RT,RP,XP,m_ref,wb,f_ref,x_ref,sems):
    top=slice(0,4*S); low=slice(4*S,NB*S)
    outs=[pltpu.make_async_copy(v.at[r],o.at[r],sems.at[i]) for i,(v,o,r) in enumerate(((f_ref,f_out,top),(x_ref,x_out,top),(f_ref,f_out,low),(x_ref,x_out,low)))]
    def zero():
        for K in range(NB):
            if K: f_ref[K*S:K*S+S,0:K*S]=jnp.zeros((S,K*S),jnp.float32)
    r_=lax.broadcasted_iota(jnp.int32,(S,S),0); c_=lax.broadcasted_iota(jnp.int32,(S,S),1)
    def tile(b): return a_ref[b*S:b*S+S,:]
    def unpack(p,ks):
        t=tile(15+p); u=jnp.transpose(t)
        if 0 in ks: A[bi(2*p,2*p)]=jnp.where(r_<=c_,t,u)
        if 1 in ks:
            v=jnp.where(r_>c_,t,u)
            A[bi(2*p+1,2*p+1)]=jnp.where(r_==c_,a_ref[18*S+p:18*S+p+1,:],v)
    def base(K,I,J):
        return tile(above(I,J)) if K==0 and I!=J else A[bi(I,J)]
    unpack(0,(0,1))
    fill=[lambda p=p: unpack(p,(0,1)) for p in (1,2)]+[lambda j=j: weave(one,two,m_ref,wb,[j]) for j in range(5)]
    def put(ref,p):
        for i in range(3): ref[i]=p[i]
    def get(ref): return ref[0],ref[1],ref[2]
    for K in range(NB):
        Dk=A.at[bi(K,K)]
        diag(Dk,T,ones,fill)
        if K==4:
            outs[0].start(); outs[1].start()
        f_ref[K*S:K*S+S,K*S:K*S+S]=Dk[...]
        put(TP,parts(T[...]))
        def panel(J,K=K):
            r=mm(left(get(TP)),right(parts(base(K,K,J))))
            f_ref[K*S:K*S+S,J*S:J*S+S]=r
            put(RT.at[J],parts(jnp.transpose(r))); put(RP.at[J],parts(r))
        def update(I,J,K=K):
            b=bi(I,J)
            A[b]=base(K,I,J)-mm(left(get(RT.at[I])),right(get(RP.at[J])))
        def solve(K=K):
            tp=get(TP)
            if K==0:
                m=m_ref[K*S:K*S+S,:]
                xk=mm(jnp.concatenate(tp,axis=1),jnp.concatenate([m,m,m],axis=0))
            else:
                xk=mm(left(tp),right(parts(M[K*S:K*S+S,:])))
            x_ref[K*S:K*S+S,:]=xk.astype(BF)
            if K<NB-1: put(XP,parts(xk))
        def updm(I,K=K):
            m0=m_ref[I*S:I*S+S,:].astype(jnp.float32) if K==0 else M[I*S:I*S+S,:]
            M[I*S:I*S+S,:]=m0-mm(left(get(RT.at[I])),right(get(XP)))
        if K==NB-1:
            solve()
            outs[2].start(); outs[3].start()
            for o in outs: o.wait()
            break
        panel(K+1)
        update(K+1,K+1)
        if K==0: fill.append(zero)
        for J in range(K+2,NB): fill.append(lambda J=J,f=panel: f(J))
        fill.append(solve)
        for I in range(K+1,NB):
            for J in range(I,NB):
                if J>K+1: fill.append(lambda I=I,J=J,f=update: f(I,J))
            fill.append(lambda I=I,f=updm: f(I))
def chol_solve(blocks,one,two):
    n=one.shape[2]
    vm=pl.BlockSpec(memory_space=pltpu.VMEM)
    return pl.pallas_call(chol_kernel,out_shape=(jax.ShapeDtypeStruct((768,768),jnp.float32),jax.ShapeDtypeStruct((768,n),jnp.bfloat16)),
        in_specs=[vm,vm,vm,vm],out_specs=(pl.BlockSpec(memory_space=pl.ANY),pl.BlockSpec(memory_space=pl.ANY)),
        scratch_shapes=[pltpu.VMEM((21,S,S),jnp.float32),pltpu.VMEM((S,S),jnp.float32),pltpu.VMEM((768,n),jnp.float32),pltpu.VMEM((3,S,S),BF),pltpu.VMEM((NB,3,S,S),BF),pltpu.VMEM((NB,3,S,S),BF),pltpu.VMEM((3,S,n),BF),pltpu.VMEM((768,n),BF),pltpu.VMEM((5,768,128),jnp.float32),pltpu.VMEM((768,768),jnp.float32),pltpu.VMEM((768,n),BF),pltpu.SemaphoreType.DMA((4,))],
        compiler_params=pltpu.CompilerParams(vmem_limit_bytes=40<<20))(blocks,one,two,jnp.ones((8,128),jnp.float32))


def body(velocity):
    slabs = 32
    forward = [(i, i + 1) for i in range(slabs - 1)]
    backward = [(i + 1, i) for i in range(slabs - 1)]
    lo = lax.ppermute(velocity[:, 1:, 1:5], ("y", "z"), forward)
    hi = lax.ppermute(velocity[:, 1:, 0:4], ("y", "z"), backward)
    share, rest = inner(velocity)
    one = lax.all_to_all(share, ("x", "c"), 0, 0, tiled=True)
    two = lax.all_to_all(outer(velocity, lo, hi, rest), ("x", "c"), 0, 0, tiled=True)
    total = total_of(gram_blocks(one, two))
    factor, modes = chol_solve(total, one, two)
    return modes.reshape(NB * S, 1, 640), factor


def solution(mesh):
    fine = Mesh(mesh.devices.reshape(4, 2, 4, 8), ("x", "c", "y", "z"))
    in_specs = (P(("x", "c"), None, ("y", "z"), None, None),)
    out_specs = (P(None, ("y", "z"), ("x", "c")), P())
    return jax.shard_map(body, mesh=fine, in_specs=in_specs, out_specs=out_specs, check_vma=False)
```
